32 devices in a mesh: groups: 2 (over x), canvas: 16 (over z, y, core).
Axes of the slice: x: 2, y: 2, z: 4, core: 2. Of those that a mesh axis runs over, the one named last changes fastest.
Arguments:
- net_slabs: int32 [65536, 2], P(('groups', 'canvas')), parts along dimension 0, may hold values from 0 to 15, all different within a row; in each aligned block of 2048 rows (0 to 2047, 2048 to 4095, ...) at most 512 rows name the same one
- row_offsets: int32 [65536, 2], P(('groups', 'canvas')), parts along dimension 0, may hold values from 0 to 15
- left_column: int32 [65536], P(('groups', 'canvas')), parts along dimension 0, may hold values from 0 to 8191
- column_span: int32 [65536], P(('groups', 'canvas')), parts along dimension 0, may hold values from 1 to 16
- pin_counts: int32 [65536], P(('groups', 'canvas')), parts along dimension 0, may hold values from 2 to 64
- tile_features: bfloat16 [7, 512, 8192], P(None, ('groups', 'canvas')), parts along dimension 1, may hold values from -6 to 6
- cotangent: float32 [512, 8192], P(('groups', 'canvas')), parts along dimension 0, may hold values from -0.0124296114 to 0.0124296114
- first_weight: bfloat16 [64, 8], replicated, may hold values from -2 to 2
- first_bias: float32 [64], replicated, may hold values from -3 to 3
- second_weight: bfloat16 [64, 64], replicated, may hold values from -0.75 to 0.75
- second_bias: float32 [64], replicated, may hold values from -3 to 3
- readout_weight: bfloat16 [64], replicated, may hold values from -0.75 to 0.75
- readout_bias: float32 [1], replicated, may hold values from -3 to 3
Outputs:
- prediction: float32 [512, 8192], P(('groups', 'canvas')), parts along dimension 0
- grad_first: float32 [128, 8], P('groups'), parts along dimension 0
- grad_first_bias: float32 [128], P('groups'), parts along dimension 0
- grad_second: float32 [128, 64], P('groups'), parts along dimension 0
- grad_second_bias: float32 [128], P('groups'), parts along dimension 0
- grad_readout: float32 [128], P('groups'), parts along dimension 0
- grad_readout_bias: float32 [2], P('groups'), parts along dimension 0
The draws below stay inside these ranges and needn't reach their ends.
There are 2 independent parts, one for each index of `groups`. The reference program is written for one: setup_inputs(seed, part) draws one part's arguments, and reference() takes and returns one part's arrays. A program takes and returns all parts, laid end to end along the dimension named above; an argument that names none is the same for every part. Nothing has to cross between parts.
Inputs may be any that keep to these rules, and one draw needn't show every extreme that they name: `net_slabs`: the two slab numbers of a net differ. Among the 2048 rows of one device no slab number is named by more than 512 rows, and in some device's rows one slab number is named by exactly 512 rows.
All inputs are finite; a program needn't handle non-finite values.
Results may differ from the reference program's by a relative error of at most 0.0071.
Values sent between devices are 32-bit elements; how exact they have to be, the bound alone decides.
A program may use at most 64 MiB of HBM per device.

```python
import math
import jax
import jax.numpy as jnp
import numpy as np
from jax import lax

ROWS_DEV = 16
W = 8192
NETS_DEV = 2048
SPAN = 16
CIN = 8
HID = 64
CF = 7
ROWS = 256
NETS = 32768
CAP = 512
N_CANVAS = 16


def draw_cotangent(key, part):
    scale = 1.0 / (ROWS * W) ** 0.5
    rising = 1.0 + 2.0 * jnp.arange(ROWS).astype(jnp.float32) / ROWS
    base = jnp.clip(jax.random.normal(key, (ROWS, W), jnp.float32), -6.0, 6.0) * scale
    return (base * rising[:, None]).astype(jnp.float32)


def set_ends(result, own_key, least, top_value):
    longest = result.shape.index(max(result.shape))
    spots = []
    for shift in (0, 1):
        where = [jax.random.randint(jax.random.fold_in(own_key, axis), (), 0, length) for axis, length in enumerate(result.shape)]
        where[longest] = (where[longest] + shift) % result.shape[longest]
        spots.append(tuple(where))
    return result.at[spots[0]].set(least).at[spots[1]].set(top_value)


def block_scale(stream_key, shape, split, smallest, largest):
    def one(dim, blocks):
        steps = jax.random.uniform(jax.random.fold_in(jax.random.fold_in(stream_key, 6), dim), (blocks,), jnp.float32, smallest / len(split), largest / len(split))
        return jnp.repeat(jnp.exp(steps), shape[dim] // blocks).reshape((-1,) + (1,) * (len(shape) - dim - 1))

    gain = one(*split[0])
    for cut in split[1:]:
        gain = gain * one(*cut)
    return gain


def deal_out(stream_key, own, number, rows, number_of, top, reach, skew):
    ranking = jax.random.permutation(stream_key, number_of)
    crowded, common = load_shares(number_of, rows * top, reach, skew, True), load_shares(number_of, rows * top, reach, skew, False)
    places = jnp.arange(number_of)

    def named(lengths, offset_by):
        used = int((lengths > 0).sum())
        fixed = max(1, used // 4)
        shifted = fixed + (places - fixed + offset_by * (used - fixed)) % max(1, number_of - fixed)
        return jnp.zeros((number_of,), jnp.int32).at[ranking[jnp.where(places < fixed, places, shifted)]].set(jnp.asarray(lengths, jnp.int32))

    lengths = jnp.where(number % 4 == 0, named(crowded, number // 4), named(common, number - number // 4 - 1))
    mixed = jax.random.permutation(jax.random.fold_in(own, 3), number_of)
    source_of, taker = mixed[0:number_of // 2 * 2:2], mixed[1:number_of // 2 * 2:2]
    margin = jnp.minimum(lengths[source_of] - 1, reach - lengths[taker]) // 2
    margin = jnp.where((source_of == ranking[0]) | (taker == ranking[0]) | (lengths[taker] == 0), 0, jnp.maximum(margin, 0))
    shifted = jax.random.randint(jax.random.fold_in(own, 4), (number_of // 2,), 0, 1 << 20) % (margin + 1)
    lengths = lengths.at[source_of].add(-shifted).at[taker].add(shifted)
    items = jnp.searchsorted(jnp.cumsum(lengths), jnp.arange(rows * top), side="right").astype(jnp.int32)
    listing = items.reshape(top, rows).T
    listing = listing[jax.random.permutation(jax.random.fold_in(own, 1), rows)]
    offset_by = jax.random.randint(jax.random.fold_in(own, 2), (rows, 1), 0, top)
    return jnp.take_along_axis(listing, (jnp.arange(top)[None, :] + offset_by) % top, axis=1)


def load_shares(amount, total, reach, lean, full):
    weights = [(1 << 20) // math.isqrt(standing ** lean) + 1 for standing in range(1, amount + 1)]
    largest = reach if full else min(reach, max(-(-total // amount), total * weights[0] // sum(weights)))
    least = 1 if total - largest >= amount - 1 else 0
    counts, surplus = [largest] + [least] * (amount - 1), total - largest - least * (amount - 1)
    while surplus > 0:
        free = [i for i in range(1, amount) if counts[i] < largest] or [i for i in range(1, amount) if counts[i] < reach]
        pool, left = sum([weights[i] for i in free]), surplus
        for i in free:
            more = min(reach - counts[i], max(1, left * weights[i] // pool), surplus)
            counts[i] = counts[i] + more
            surplus = surplus - more
    return np.array(counts)


def bell_draw(stream_key, extent, scale, bound, shards=(), dtype=jnp.bfloat16):
    values = jax.random.normal(stream_key, extent, jnp.float32) * scale
    if len(shards) > 0:
        values = block_scale(stream_key, extent, shards, -0.22, 0.18) * values
    return jnp.clip(values, min=-bound, max=bound).astype(dtype)


def setup_inputs(seed: int = 0, part: int = 0) -> dict:
    arg_keys = jax.random.split(jax.random.key(seed), 14)
    part_splits = jax.random.split(jax.random.fold_in(arg_keys[13], part), 14)
    net_slabs_keys = jax.random.split(jax.random.fold_in(part_splits[0], 1), NETS // NETS_DEV)
    net_slabs_turns = jax.random.permutation(jax.random.fold_in(part_splits[0], 3), NETS // NETS_DEV)
    net_slabs = jax.vmap(lambda own, number: deal_out(jax.random.fold_in(part_splits[0], 2), own, number, NETS_DEV, N_CANVAS, 2, CAP, 1))(net_slabs_keys, net_slabs_turns).reshape((NETS, 2))
    row_offsets = set_ends(jax.random.randint(part_splits[1], (NETS, 2), 0, ROWS_DEV), jax.random.fold_in(part_splits[1], 1), 0, ROWS_DEV - 1).astype(jnp.int32)
    left_column = set_ends(jax.random.randint(part_splits[2], (NETS,), 0, W), jax.random.fold_in(part_splits[2], 1), 0, W - 1).astype(jnp.int32)
    column_span = set_ends(jax.random.randint(part_splits[3], (NETS,), 1, SPAN + 1), jax.random.fold_in(part_splits[3], 1), 1, SPAN).astype(jnp.int32)
    pin_counts = set_ends(jax.random.randint(part_splits[4], (NETS,), 2, 65), jax.random.fold_in(part_splits[4], 1), 2, 64).astype(jnp.int32)
    tile_features = bell_draw(part_splits[5], (CF, ROWS, W), 1.0, 6.0, ((1, 16),))
    cotangent = draw_cotangent(jax.random.fold_in(jax.random.fold_in(arg_keys[13], part), 71), part)
    first_weight = bell_draw(arg_keys[7], (HID, CIN), CIN ** -0.5, 2.0)
    first_bias = bell_draw(arg_keys[8], (HID,), 0.5, 3.0, (), jnp.float32)
    second_weight = bell_draw(arg_keys[9], (HID, HID), HID ** -0.5, 0.75)
    second_bias = bell_draw(arg_keys[10], (HID,), 0.5, 3.0, (), jnp.float32)
    readout_weight = bell_draw(arg_keys[11], (HID,), HID ** -0.5, 0.75)
    readout_bias = bell_draw(arg_keys[12], (1,), 1.0, 3.0, (), jnp.float32)
    return dict(net_slabs=net_slabs, row_offsets=row_offsets, left_column=left_column, column_span=column_span, pin_counts=pin_counts, tile_features=tile_features, cotangent=cotangent, first_weight=first_weight, first_bias=first_bias, second_weight=second_weight, second_bias=second_bias, readout_weight=readout_weight, readout_bias=readout_bias)


root_half = 0.7071067811865476
inv_root_tau = 0.3989422804014327

def gelu_value(value):
    return 0.5 * value * (1.0 + jax.scipy.special.erf(value * root_half))

def gelu_slope(value):
    return 0.5 * (1.0 + jax.scipy.special.erf(value * root_half)) + value * jnp.exp(-0.5 * value * value) * inv_root_tau

def cell_block(inputs, grad_row, first_weight, first_bias, second_weight, second_bias, readout_weight, readout_bias):
    first_pre = jnp.dot(first_weight, inputs, preferred_element_type=jnp.float32) + first_bias[:, None]
    act_one = gelu_value(first_pre).astype(jnp.bfloat16)
    second_pre = jnp.dot(second_weight, act_one, preferred_element_type=jnp.float32) + second_bias[:, None]
    act_two = gelu_value(second_pre).astype(jnp.bfloat16)
    prediction = jnp.dot(readout_weight[None, :], act_two, preferred_element_type=jnp.float32)[0] + readout_bias[0]
    grad_readout = lax.optimization_barrier(jnp.sum(act_two.astype(jnp.float32) * grad_row[None, :], axis=1))
    grad_readout_bias = jnp.sum(grad_row).reshape(1)
    delta_two_full = readout_weight.astype(jnp.float32)[:, None] * grad_row[None, :] * gelu_slope(second_pre)
    delta_two = delta_two_full.astype(jnp.bfloat16)
    grad_second = jnp.dot(delta_two, act_one.T, preferred_element_type=jnp.float32)
    grad_second_bias = lax.optimization_barrier(jnp.sum(delta_two_full, axis=1))
    back_one = jnp.dot(second_weight.T, delta_two, preferred_element_type=jnp.float32)
    delta_one_full = back_one * gelu_slope(first_pre)
    delta_one = delta_one_full.astype(jnp.bfloat16)
    grad_first = jnp.dot(delta_one, inputs.T, preferred_element_type=jnp.float32)
    grad_first_bias = lax.optimization_barrier(jnp.sum(delta_one_full, axis=1))
    return (prediction, (grad_first, grad_first_bias, grad_second, grad_second_bias, grad_readout, grad_readout_bias))

def reference(net_slabs, row_offsets, left_column, column_span, pin_counts, tile_features, cotangent, first_weight, first_bias, second_weight, second_bias, readout_weight, readout_bias):
    first_is_low = net_slabs[:, 0] <= net_slabs[:, 1]
    low_slab = jnp.minimum(net_slabs[:, 0], net_slabs[:, 1])
    high_slab = jnp.maximum(net_slabs[:, 0], net_slabs[:, 1])
    low_offset = jnp.where(first_is_low, row_offsets[:, 0], row_offsets[:, 1])
    high_offset = jnp.where(first_is_low, row_offsets[:, 1], row_offsets[:, 0])
    bottom_row = (low_slab * ROWS_DEV + low_offset).astype(jnp.int32)
    top_row = (high_slab * ROWS_DEV + high_offset).astype(jnp.int32)
    right_edge = jnp.minimum(left_column + column_span, W).astype(jnp.int32)
    span_columns = (right_edge - left_column).astype(jnp.float32)
    span_rows = (top_row - bottom_row).astype(jnp.float32)
    net_weight = jnp.sqrt(pin_counts.astype(jnp.float32)) * (span_columns + span_rows) / (span_columns * span_rows)
    edges = jnp.zeros((ROWS, W + 1), jnp.float32)
    edges = edges.at[bottom_row, left_column].add(net_weight)
    edges = edges.at[bottom_row, right_edge].add(-net_weight)
    edges = edges.at[top_row, left_column].add(-net_weight)
    edges = edges.at[top_row, right_edge].add(net_weight)
    across = jnp.cumsum(edges[:, :W], axis=1)
    demand = jnp.cumsum(across, axis=0)
    level = jnp.log1p(demand).astype(jnp.bfloat16)

    def row_step(totals, row_index):
        inputs = jnp.concatenate([level[row_index][None, :], tile_features[:, row_index, :]], axis=0)
        prediction, grads = cell_block(inputs, cotangent[row_index], first_weight, first_bias, second_weight, second_bias, readout_weight, readout_bias)
        return (tuple((a + b for a, b in zip(totals, grads))), prediction)
    start = (jnp.zeros((HID, CIN), jnp.float32), jnp.zeros((HID,), jnp.float32), jnp.zeros((HID, HID), jnp.float32), jnp.zeros((HID,), jnp.float32), jnp.zeros((HID,), jnp.float32), jnp.zeros((1,), jnp.float32))
    totals, prediction = lax.scan(row_step, start, jnp.arange(ROWS).astype(jnp.int32))
    return (prediction, totals[0], totals[1], totals[2], totals[3], totals[4], totals[5])
```

```python
import functools
import jax
import jax.numpy as jnp
from jax import lax
from jax.experimental import pallas as pl
from jax.experimental.pallas import tpu as pltpu
from jax.sharding import PartitionSpec as P

root_half = 0.7071067811865476
log2_two_over_root_pi = 0.17425071
log2e = 1.4426950408889634
f32 = jnp.float32
bf16 = jnp.bfloat16
i32 = jnp.int32
NT = (((1,), (1,)), ((), ()))


def iota(shape, dim):
    return lax.broadcasted_iota(i32, shape, dim)


def lanes(a):
    return sum(a[:, k * 128 : (k + 1) * 128] for k in range(a.shape[1] // 128))


def gelu_parts(v):
    w = v * root_half
    both = 1.0 + lax.erf(w)
    w = w.astype(bf16)
    tail = w * jnp.exp2((w * w) * bf16(-log2e) + bf16(log2_two_over_root_pi))
    return (v * both).astype(bf16), both, tail


def split_column(b):
    high = b.astype(bf16).astype(f32)
    return high, b - high


def mlp_body(chunk, demand_ref, base_ref, feat_ref, cot_ref, w1_ref, b1_ref, w2_ref, b2_ref, ro_ref, rb_ref,
             pred_ref, grads_ref,
             w1p, w2x, w2t, rox, move, xs, xp, acc1, acc2, accc):
    step = pl.program_id(0)
    slab_rows, width = demand_ref.shape
    hidden, cin = w1_ref.shape
    pair = 2 * hidden
    pairs = slab_rows // 2
    depth = cin * slab_rows
    deep = 4 * cin
    half = 2 * cin
    reach = xs.shape[0]

    @pl.when(step == 0)
    def _():
        pick = (iota((pair, hidden), 0) % hidden == iota((pair, hidden), 1)).astype(bf16)
        pick_f = pick.astype(f32)
        spread = (iota((cin, deep), 1) // 2 == iota((cin, deep), 0)).astype(bf16)
        tall = jnp.dot(pick, w1_ref[...], preferred_element_type=f32).astype(bf16)
        wide = jnp.dot(tall, spread, preferred_element_type=f32)
        high, low = split_column(jnp.sum(pick_f * b1_ref[...], axis=1, keepdims=True))
        lane = iota((pair, deep), 1)
        keep = iota((pair, deep), 0) // hidden == lane % 2
        w1p[...] = jnp.where(
            lane == half, high, jnp.where(lane == half + 1, low, jnp.where(keep, wide, 0.0))).astype(bf16)
        same = iota((pair, pair), 0) // hidden == iota((pair, pair), 1) // hidden
        down = jnp.dot(pick, w2_ref[...], preferred_element_type=f32).astype(bf16)
        full = lax.dot_general(down, pick, NT, preferred_element_type=f32)
        w2x[:, 0:pair] = jnp.where(same, 0.5 * full, 0.0).astype(bf16)
        high, low = split_column(jnp.sum(pick_f * b2_ref[...], axis=1, keepdims=True))
        lane = iota((pair, 128), 1)
        w2x[:, pair : pair + 128] = jnp.where(lane == 0, high, jnp.where(lane == 1, low, 0.0)).astype(bf16)
        flip = lax.dot_general(pick, w2_ref[...], NT, preferred_element_type=f32).astype(bf16)
        full_t = lax.dot_general(flip, pick, NT, preferred_element_type=f32)
        ro_wide = lax.dot_general(ro_ref[...], pick, NT, preferred_element_type=f32)
        w2t[...] = jnp.where(same, 0.25 * full_t * ro_wide, 0.0).astype(bf16)
        ro_rows = 0.5 * jnp.broadcast_to(ro_wide, (slab_rows, pair))
        for p in range(pairs):
            here = iota((slab_rows, pair), 0) == iota((slab_rows, pair), 1) // hidden + 2 * p
            rox[p] = jnp.where(here, ro_rows, 0.0).astype(bf16)
        line = iota((pairs * deep, reach), 0)
        slot = line % deep
        row = 2 * (line // deep) + slot % 2
        source = jnp.where(slot < half, (slot // 2) * slab_rows + row,
                           jnp.where(slot < half + 2, depth + 2 * slab_rows,
                                     jnp.where(slot < half + 6, depth + (slot // 2 - cin - 1) * slab_rows + row, -1)))
        move[...] = (iota((pairs * deep, reach), 1) == source).astype(bf16)
        acc1[...] = jnp.zeros_like(acc1)
        acc2[...] = jnp.zeros_like(acc2)
        accc[...] = jnp.zeros_like(accc)
        xs[depth + 2 * slab_rows : reach, :] = jnp.ones((reach - depth - 2 * slab_rows, width), bf16)

    cots = cot_ref[...]
    cot_high = cots.astype(bf16)
    xs[0:slab_rows, :] = jnp.log(1.0 + (demand_ref[...] + base_ref[...])).astype(bf16)
    xs[slab_rows:depth, :] = feat_ref[...].reshape((cin - 1) * slab_rows, width)
    xs[depth : depth + slab_rows, :] = cot_high
    xs[depth + slab_rows : depth + 2 * slab_rows, :] = (cots - cot_high.astype(f32)).astype(bf16)
    accc[...] += lanes(cots)
    chunks = width // chunk
    units = pairs * chunks
    for q in range(chunks):
        cols = slice(q * chunk, (q + 1) * chunk)
        xp[:, cols] = jnp.dot(move[...], xs[:, cols], preferred_element_type=f32).astype(bf16)
    ones = jnp.ones((slab_rows, chunk), bf16)
    v1, a1, s1, v2, d2, a2, back, d1 = {}, {}, {}, {}, {}, {}, {}, {}

    def x_of(u):
        p, q = divmod(u, chunks)
        return xp[p * deep : (p + 1) * deep, q * chunk : (q + 1) * chunk]

    def first(u):
        v1[u] = jnp.dot(w1p[...], x_of(u), preferred_element_type=f32)

    def first_gelu(u):
        a, both, tail = gelu_parts(v1.pop(u))
        a1[u] = jnp.concatenate([a, ones], axis=0)
        s1[u] = both + tail.astype(f32)

    def second(u):
        v2[u] = jnp.dot(w2x[:, 0 : pair + slab_rows], a1[u], preferred_element_type=f32)

    def second_gelu(u):
        p, q = divmod(u, chunks)
        a2[u], both, tail = gelu_parts(v2.pop(u))
        cot = jnp.concatenate([
            jnp.broadcast_to(cot_ref[2 * p + k : 2 * p + k + 1, q * chunk : (q + 1) * chunk], (hidden, chunk))
            for k in range(2)], axis=0)
        d2[u] = (cot * (both + tail.astype(f32))).astype(bf16)

    def third(u):
        p, q = divmod(u, chunks)
        back[u] = jnp.dot(w2t[...], d2[u], preferred_element_type=f32)
        part = jnp.dot(rox[p], a2[u], preferred_element_type=f32)
        cols = slice(q * chunk, (q + 1) * chunk)
        if p == 0:
            pred_ref[:, cols] = part + rb_ref[0, 0]
        else:
            pred_ref[:, cols] += part
        if q == chunks - 1:
            mine = range(u - chunks + 1, u + 1)
            acc2[...] += lax.dot_general(
                jnp.concatenate([d2.pop(k) for k in mine], axis=1), jnp.concatenate([a1.pop(k) for k in mine], axis=1),
                NT, preferred_element_type=f32)

    def third_slope(u):
        d1[u] = (back.pop(u) * s1.pop(u)).astype(bf16)

    def fourth(u):
        if u % chunks == chunks - 1:
            mine = range(u - chunks + 1, u + 1)
            both = [jnp.concatenate([d1.pop(k), a2.pop(k)], axis=0) for k in mine]
            acc1[...] += lax.dot_general(
                jnp.concatenate([x_of(k) for k in mine], axis=1), jnp.concatenate(both, axis=1),
                NT, preferred_element_type=f32)

    for i in range(-3, units + 3):
        for stage, lag in ((first, 3), (second_gelu, 0), (second, 1), (first_gelu, 2), (third, -1), (third_slope, -2),
                           (fourth, -3)):
            if 0 <= i + lag < units:
                stage(i + lag)

    @pl.when(step == pl.num_programs(0) - 1)
    def _():
        total2 = acc2[...]
        g2 = total2[0:hidden, 0:hidden] + total2[hidden:pair, hidden:pair]
        ro = jnp.sum((iota((hidden, hidden), 0) == iota((hidden, hidden), 1)).astype(f32) * ro_ref[...].astype(f32),
                     axis=1, keepdims=True)
        g2 = 0.25 * ro * g2
        gb2 = 0.5 * ro * (total2[0:hidden, pair : pair + 1] + total2[hidden:pair, pair : pair + 1])
        flat = acc1[...]
        slot = iota((deep, pair), 0)
        side = iota((deep, pair), 1) // hidden
        keep = ((slot % 2 == side) & (slot < half)) | (slot == half)
        weights = jnp.where(keep, flat[:, 0:pair], 0.0)
        reads = jnp.where((slot % 2 == side) & (slot > half + 1), flat[:, pair : 2 * pair], 0.0)
        fold = (iota((pair, hidden), 0) % hidden == iota((pair, hidden), 1)).astype(f32)
        lane = iota((deep, hidden), 1)
        row = iota((deep, hidden), 0)
        place = (lane == jnp.where(row <= half, row // 2, -1)).astype(f32)
        place_r = ((lane == cin + 1) & (row > half + 1)).astype(f32)
        TN = (((0,), (0,)), ((), ()))
        exact = dict(precision=lax.Precision.HIGHEST, preferred_element_type=f32)
        up = jnp.dot(weights, fold, **exact)
        up_r = 0.5 * jnp.dot(reads, fold, **exact)
        g1 = lax.dot_general(up, place, TN, **exact) + lax.dot_general(up_r, place_r, TN, **exact)
        gb3 = jnp.sum(accc[...], keepdims=True)
        lane = iota((hidden, hidden), 1)
        right = jnp.where(lane == cin + 2, gb2, jnp.where(lane == cin + 3, gb3, g1))
        packed = jnp.concatenate([g2, right], axis=1)
        n, k, _ = grads_ref.shape
        for j in range(n):
            grads_ref[j] = packed[j * k : (j + 1) * k]


def mlp(demand, base, feats, cot, w1, b1, w2, b2, ro, rb, devices, width=1024, chunk=256):
    slab_rows, w = demand.shape
    hidden, cin = w1.shape
    pair = 2 * hidden
    depth = cin * slab_rows
    whole = lambda s: pl.BlockSpec(s, lambda i: tuple(0 for _ in s))
    cols = pl.BlockSpec((slab_rows, width), lambda i: (0, i))
    return pl.pallas_call(
        functools.partial(mlp_body, chunk),
        grid=(w // width,),
        in_specs=[
            cols, pl.BlockSpec((1, width), lambda i: (0, i)),
            pl.BlockSpec((cin - 1, slab_rows, width), lambda i: (0, 0, i)), cols,
            whole((hidden, cin)), whole((1, hidden)), whole((hidden, hidden)), whole((1, hidden)), whole((1, hidden)),
            pl.BlockSpec(memory_space=pltpu.SMEM),
        ],
        out_specs=[cols, whole((devices, hidden // devices, 2 * hidden))],
        out_shape=[
            jax.ShapeDtypeStruct((slab_rows, w), f32),
            jax.ShapeDtypeStruct((devices, hidden // devices, 2 * hidden), f32),
        ],
        scratch_shapes=[
            pltpu.VMEM((pair, 4 * cin), bf16),
            pltpu.VMEM((pair, pair + 128), bf16),
            pltpu.VMEM((pair, pair), bf16),
            pltpu.VMEM((slab_rows // 2, slab_rows, pair), bf16),
            pltpu.VMEM((2 * cin * slab_rows, depth + 3 * slab_rows), bf16),
            pltpu.VMEM((depth + 3 * slab_rows, width), bf16),
            pltpu.VMEM((2 * cin * slab_rows, width), bf16),
            pltpu.VMEM((4 * cin, 2 * pair), f32),
            pltpu.VMEM((pair, pair + slab_rows), f32),
            pltpu.VMEM((slab_rows, 128), f32),
        ],
        compiler_params=pltpu.CompilerParams(vmem_limit_bytes=40 * 1024 * 1024),
        name="mlp",
    )(demand, base, feats, cot, w1, b1[None, :], w2, b2[None, :], ro[None, :], rb[None, :])


def greet(n):
    me, group = lax.axis_index("canvas"), lax.axis_index("groups")
    barrier = pltpu.get_barrier_semaphore()

    def hail(k, carry):
        pl.semaphore_signal(
            barrier, inc=1, device_id=(group, lax.rem(me + k, n)), device_id_type=pl.DeviceIdType.MESH)
        return carry

    lax.fori_loop(1, n, hail, 0)
    pl.semaphore_wait(barrier, n - 1)


def swap(n, source, target, send_sem, recv_sem):
    me, group = lax.axis_index("canvas"), lax.axis_index("groups")

    def copy(k, slot):
        peer = lax.rem(me + k, n)
        return pltpu.make_async_remote_copy(
            src_ref=source.at[peer], dst_ref=target.at[slot], send_sem=send_sem.at[k], recv_sem=recv_sem.at[k],
            device_id=(group, peer), device_id_type=pl.DeviceIdType.MESH)

    def start(k, carry):
        copy(k, me).start()
        return carry

    def arrive(k, carry):
        copy(k, lax.rem(me + n - k, n)).wait_recv()
        return carry

    lax.fori_loop(1, n, start, 0)
    target[pl.ds(me, 1)] = source[pl.ds(me, 1)]
    lax.fori_loop(1, n, arrive, 0)

    def finish():
        def left(k, carry):
            copy(k, me).wait_send()
            return carry

        lax.fori_loop(1, n, left, 0)

    return finish


def route_body(n, lane_group, send_ref, local_ref, base_ref, items, acc, totals, got, result, back,
               send_a, recv_a, send_b, recv_b, send_c, recv_c):
    greet(n)
    end_a = swap(n, send_ref, items, send_a, recv_a)
    slab(lane_group, items, local_ref, totals, acc)
    end_b = swap(n, totals, got, send_b, recv_b)
    running = jnp.zeros(got.shape[1:], f32)
    for d in range(n):
        result[d] = running
        running = running + got[d]
    end_c = swap(n, result, back, send_c, recv_c)
    part = got.shape[2]
    for d in range(n):
        base_ref[:, d * part : (d + 1) * part] = back[d]
    end_a()
    end_b()
    end_c()


def route(send, slab_rows, w, lane_group=256):
    n = send.shape[0]
    vmem = pl.BlockSpec(memory_space=pltpu.VMEM)
    part = pltpu.VMEM((n, 1, w // n), f32)
    return pl.pallas_call(
        functools.partial(route_body, n, lane_group),
        out_shape=[jax.ShapeDtypeStruct((slab_rows, w), f32), jax.ShapeDtypeStruct((1, w), f32)],
        in_specs=[vmem],
        out_specs=[vmem] * 2,
        scratch_shapes=[
            pltpu.VMEM(send.shape, f32), pltpu.VMEM((slab_rows * w // lane_group, 2 * lane_group + 256), f32),
            part, part, part, part,
        ] + [pltpu.SemaphoreType.DMA((n,))] * 6,
        compiler_params=pltpu.CompilerParams(collective_id=0, has_side_effects=True),
        name="route",
    )(send)


def sum_body(n, grads_ref, total_ref, got, result, back, send_a, recv_a, send_b, recv_b):
    greet(n)
    end_a = swap(n, grads_ref, got, send_a, recv_a)
    total = got[0]
    for d in range(1, n):
        total = total + got[d]
    for d in range(n):
        result[d] = total
    end_b = swap(n, result, back, send_b, recv_b)
    k = got.shape[1]
    for d in range(n):
        total_ref[d * k : (d + 1) * k, :] = back[d]
    end_a()
    end_b()


def split_body(total_ref, g1_out, gb1_out, g2_out, gb2_out, gr_out, gb_out,
               g1_ref, gb1_ref, g2_ref, gb2_ref, gr_ref, gb_ref, out_sem):
    cin, hidden = g1_ref.shape
    g2_ref[...] = total_ref[:, 0:hidden]
    right = total_ref[:, hidden:]
    eye = iota((hidden, hidden), 0) == iota((hidden, hidden), 1)

    def row(lane):
        return jnp.sum(jnp.where(eye, right[:, lane : lane + 1], 0.0), axis=0, keepdims=True)

    g1_ref[...] = jnp.concatenate([row(c) for c in range(cin)], axis=0)
    gb1_ref[...] = row(cin).reshape(hidden)
    gr_ref[...] = row(cin + 1).reshape(hidden)
    gb2_ref[...] = row(cin + 2).reshape(hidden)
    gb_ref[...] = right[0:1, cin + 3 : cin + 4].reshape(1)
    pairs = ((g1_ref, g1_out), (gb1_ref, gb1_out), (g2_ref, g2_out), (gb2_ref, gb2_out), (gr_ref, gr_out),
             (gb_ref, gb_out))
    copies = [pltpu.make_async_copy(source, target, out_sem.at[i]) for i, (source, target) in enumerate(pairs)]
    for c in copies:
        c.start()
    for c in copies:
        c.wait()


def sum_all(grads, cin):
    n, k, _ = grads.shape
    hidden = n * k
    vmem = pl.BlockSpec(memory_space=pltpu.VMEM)
    line = (hidden,)
    shapes = ((cin, hidden), line, (hidden, hidden), line, line, (1,))
    total = linked(sum_body, n, grads, (hidden, 2 * hidden), 2, 1, "sum_all")
    return pl.pallas_call(
        split_body,
        out_shape=[jax.ShapeDtypeStruct(shape, f32) for shape in shapes],
        in_specs=[vmem],
        out_specs=[pl.BlockSpec(memory_space=pltpu.HBM)] * 6,
        scratch_shapes=[pltpu.VMEM(shape, f32) for shape in shapes] + [pltpu.SemaphoreType.DMA((6,))],
        name="split",
    )(total)


def linked(body, n, x, out_shape, phases, collective_id, name):
    vmem = pl.BlockSpec(memory_space=pltpu.VMEM)
    extra = [pltpu.VMEM(x.shape, f32)] * 3 if phases == 2 else []
    return pl.pallas_call(
        functools.partial(body, n),
        out_shape=jax.ShapeDtypeStruct(out_shape, f32),
        in_specs=[vmem],
        out_specs=vmem,
        scratch_shapes=extra + [pltpu.SemaphoreType.DMA((n,))] * (2 * phases),
        compiler_params=pltpu.CompilerParams(collective_id=collective_id, has_side_effects=True),
        name=name,
    )(x)


def slab(lane_group, got_ref, local_ref, totals_ref, acc):
    n, _, cap = got_ref.shape
    slab_rows, w = local_ref.shape
    tail = 128
    per = max(1, min(n, 2048 // cap))
    for c in range(n // per):
        def line(which):
            return jnp.concatenate([got_ref[c * per + j, which : which + 1, :] for j in range(per)], axis=1)

        value = line(0)
        place = line(1).astype(i32)
        end = line(2).astype(i32)
        row = place // w
        start = place - row * w
        group = start // lane_group
        first = start - group * lane_group
        last = end - group * lane_group
        key = group * slab_rows + row
        limit = (group + 1) * slab_rows
        hi = value.astype(bf16).astype(f32)
        lo = value - hi
        count = per * cap
        m = iota((acc.shape[0], count), 0)
        hot = jnp.where((m >= key) & (m < limit), 1.0, 0.0).astype(bf16)
        lane = iota((lane_group, count), 0)
        inside = (lane >= first) & (lane < last)
        over = (iota((tail, count), 0) + lane_group) < last
        fine = jnp.concatenate(
            [jnp.where(inside, hi, 0.0).astype(bf16), jnp.where(inside, lo, 0.0).astype(bf16),
             jnp.where(over, hi, 0.0).astype(bf16), jnp.where(over, lo, 0.0).astype(bf16)], axis=0)
        update = lax.dot_general(hot, fine, NT, preferred_element_type=f32)
        if c == 0:
            acc[...] = update
        else:
            acc[...] += update
    g2 = 2 * lane_group
    for q in range(w // lane_group):
        rows = slice(q * slab_rows, (q + 1) * slab_rows)
        main = acc[rows, 0:lane_group] + acc[rows, lane_group:g2]
        local_ref[:, q * lane_group : (q + 1) * lane_group] = main
        if q > 0:
            before = slice((q - 1) * slab_rows, q * slab_rows)
            spill = acc[before, g2 : g2 + tail] + acc[before, g2 + tail : g2 + 2 * tail]
            local_ref[:, q * lane_group : q * lane_group + tail] = main[:, 0:tail] + spill
    part = w // n
    for d in range(n):
        totals_ref[d] = local_ref[slab_rows - 1 : slab_rows, d * part : (d + 1) * part]


def per_device(
    net_slabs,
    row_offsets,
    left_column,
    column_span,
    pin_counts,
    tile_features,
    cotangent,
    first_weight,
    first_bias,
    second_weight,
    second_bias,
    readout_weight,
    readout_bias,
):
    devices = lax.axis_size("canvas")
    slab_rows = tile_features.shape[1]
    canvas_width = tile_features.shape[2]
    nets_here = pin_counts.shape[0]
    capacity = 4 * nets_here // devices
    first_is_low = net_slabs[:, 0] <= net_slabs[:, 1]
    low_slab = jnp.minimum(net_slabs[:, 0], net_slabs[:, 1])
    high_slab = jnp.maximum(net_slabs[:, 0], net_slabs[:, 1])
    low_offset = jnp.where(first_is_low, row_offsets[:, 0], row_offsets[:, 1])
    high_offset = jnp.where(first_is_low, row_offsets[:, 1], row_offsets[:, 0])
    right_edge = jnp.minimum(left_column + column_span, canvas_width)
    span_columns = (right_edge - left_column).astype(jnp.float32)
    span_rows = ((high_slab - low_slab) * slab_rows + high_offset - low_offset).astype(jnp.float32)
    net_weight = (
        jnp.sqrt(pin_counts.astype(jnp.float32))
        * (span_columns + span_rows)
        / (span_columns * span_rows)
    )
    target_slab = jnp.concatenate([low_slab, high_slab])
    local_row = jnp.concatenate([low_offset, high_offset])
    start_column = jnp.concatenate([left_column, left_column])
    end_column = jnp.concatenate([right_edge, right_edge])
    amounts = jnp.concatenate([net_weight, -net_weight])
    item_count = target_slab.shape[0]
    highest = lax.Precision.HIGHEST
    slab_ids = jnp.arange(devices, dtype=jnp.int32)
    slab_hot = (target_slab[:, None] == slab_ids[None, :]).astype(jnp.bfloat16)
    block_len = 128
    block_count = item_count // block_len
    blocked_hot = slab_hot.reshape(block_count, block_len, devices)
    lower_ones = (jnp.arange(block_len)[:, None] >= jnp.arange(block_len)[None, :]).astype(
        jnp.bfloat16
    )
    inclusive = jnp.einsum(
        "ij,bjd->bid", lower_ones, blocked_hot, preferred_element_type=jnp.float32
    )
    block_totals = inclusive[:, -1, :]
    block_start = jnp.cumsum(block_totals, axis=0) - block_totals
    counted = (inclusive + block_start[:, None, :] - 1.0) * blocked_hot.astype(jnp.float32)
    slot_rank = jnp.sum(counted, axis=2).reshape(item_count).astype(jnp.int32)
    payload = jnp.stack(
        [
            amounts,
            (local_row * canvas_width + start_column).astype(jnp.float32),
            end_column.astype(jnp.float32),
        ]
    )
    dest_mask = (slab_ids[:, None] == target_slab[None, :]).astype(jnp.float32)
    left_side = (dest_mask[:, None, :] * payload[None, :, :]).reshape(3 * devices, item_count)
    rank_hot = (slot_rank[:, None] == jnp.arange(capacity, dtype=jnp.int32)[None, :]).astype(
        jnp.float32
    )
    send_items = jnp.dot(
        left_side, rank_hot, precision=highest, preferred_element_type=jnp.float32
    ).reshape(devices, 3, capacity)
    local, base = route(send_items, slab_rows, canvas_width)
    prediction, grads = mlp(
        local, base, tile_features, cotangent, first_weight, first_bias, second_weight, second_bias,
        readout_weight, readout_bias, devices)
    g1, gb1, g2, gb2, gr, gb = sum_all(grads, first_weight.shape[1])
    return (prediction, g1.T, gb1, g2, gb2, gr, gb)


def solution(mesh):
    in_specs = (
        P(("groups", "canvas"), None),
        P(("groups", "canvas"), None),
        P(("groups", "canvas")),
        P(("groups", "canvas")),
        P(("groups", "canvas")),
        P(None, ("groups", "canvas"), None),
        P(("groups", "canvas"), None),
        P(),
        P(),
        P(),
        P(),
        P(),
        P(),
    )
    out_specs = (
        P(("groups", "canvas"), None),
        P("groups", None),
        P("groups"),
        P("groups", None),
        P("groups"),
        P("groups"),
        P("groups"),
    )
    return jax.shard_map(
        per_device, mesh=mesh, in_specs=in_specs, out_specs=out_specs, check_vma=False
    )
```

```python
import functools
import jax
import jax.numpy as jnp
from jax import lax
from jax.experimental import pallas as pl
from jax.experimental.pallas import tpu as pltpu
from jax.sharding import PartitionSpec as P

root_half = 0.7071067811865476
log2_two_over_root_pi = 0.17425071
log2e = 1.4426950408889634
f32 = jnp.float32
bf16 = jnp.bfloat16
i32 = jnp.int32
NT = (((1,), (1,)), ((), ()))


def iota(shape, dim):
    return lax.broadcasted_iota(i32, shape, dim)


def lanes(a):
    return sum(a[:, k * 128 : (k + 1) * 128] for k in range(a.shape[1] // 128))


def gelu_parts(v):
    w = v * root_half
    both = 1.0 + lax.erf(w)
    w = w.astype(bf16)
    tail = w * jnp.exp2((w * w) * bf16(-log2e) + bf16(log2_two_over_root_pi))
    return (v * both).astype(bf16), both, tail


def split_column(b):
    high = b.astype(bf16).astype(f32)
    return high, b - high


def mlp_body(chunk, demand_ref, base_ref, feat_ref, cot_ref, w1_ref, b1_ref, w2_ref, b2_ref, ro_ref, rb_ref,
             pred_ref, grads_ref,
             w1p, w2x, w2t, rox, move, xs, xp, acc1, acc2, accc):
    step = pl.program_id(0)
    slab_rows, width = demand_ref.shape
    hidden, cin = w1_ref.shape
    pair = 2 * hidden
    pairs = slab_rows // 2
    depth = cin * slab_rows
    deep = 4 * cin
    half = 2 * cin
    reach = xs.shape[0]

    @pl.when(step == 0)
    def _():
        pick = (iota((pair, hidden), 0) % hidden == iota((pair, hidden), 1)).astype(bf16)
        pick_f = pick.astype(f32)
        spread = (iota((cin, deep), 1) // 2 == iota((cin, deep), 0)).astype(bf16)
        tall = jnp.dot(pick, w1_ref[...], preferred_element_type=f32).astype(bf16)
        wide = jnp.dot(tall, spread, preferred_element_type=f32)
        high, low = split_column(jnp.sum(pick_f * b1_ref[...], axis=1, keepdims=True))
        lane = iota((pair, deep), 1)
        keep = iota((pair, deep), 0) // hidden == lane % 2
        w1p[...] = jnp.where(
            lane == half, high, jnp.where(lane == half + 1, low, jnp.where(keep, wide, 0.0))).astype(bf16)
        same = iota((pair, pair), 0) // hidden == iota((pair, pair), 1) // hidden
        down = jnp.dot(pick, w2_ref[...], preferred_element_type=f32).astype(bf16)
        full = lax.dot_general(down, pick, NT, preferred_element_type=f32)
        w2x[:, 0:pair] = jnp.where(same, 0.5 * full, 0.0).astype(bf16)
        high, low = split_column(jnp.sum(pick_f * b2_ref[...], axis=1, keepdims=True))
        lane = iota((pair, 128), 1)
        w2x[:, pair : pair + 128] = jnp.where(lane == 0, high, jnp.where(lane == 1, low, 0.0)).astype(bf16)
        flip = lax.dot_general(pick, w2_ref[...], NT, preferred_element_type=f32).astype(bf16)
        full_t = lax.dot_general(flip, pick, NT, preferred_element_type=f32)
        ro_wide = lax.dot_general(ro_ref[...], pick, NT, preferred_element_type=f32)
        w2t[...] = jnp.where(same, 0.25 * full_t * ro_wide, 0.0).astype(bf16)
        ro_rows = 0.5 * jnp.broadcast_to(ro_wide, (slab_rows, pair))
        for p in range(pairs):
            here = iota((slab_rows, pair), 0) == iota((slab_rows, pair), 1) // hidden + 2 * p
            rox[p] = jnp.where(here, ro_rows, 0.0).astype(bf16)
        line = iota((pairs * deep, reach), 0)
        slot = line % deep
        row = 2 * (line // deep) + slot % 2
        source = jnp.where(slot < half, (slot // 2) * slab_rows + row,
                           jnp.where(slot < half + 2, depth + 2 * slab_rows,
                                     jnp.where(slot < half + 6, depth + (slot // 2 - cin - 1) * slab_rows + row, -1)))
        move[...] = (iota((pairs * deep, reach), 1) == source).astype(bf16)
        acc1[...] = jnp.zeros_like(acc1)
        acc2[...] = jnp.zeros_like(acc2)
        accc[...] = jnp.zeros_like(accc)
        xs[depth + 2 * slab_rows : reach, :] = jnp.ones((reach - depth - 2 * slab_rows, width), bf16)

    cots = cot_ref[...]
    cot_high = cots.astype(bf16)
    xs[0:slab_rows, :] = jnp.log(1.0 + (demand_ref[...] + base_ref[...])).astype(bf16)
    xs[slab_rows:depth, :] = feat_ref[...].reshape((cin - 1) * slab_rows, width)
    xs[depth : depth + slab_rows, :] = cot_high
    xs[depth + slab_rows : depth + 2 * slab_rows, :] = (cots - cot_high.astype(f32)).astype(bf16)
    accc[...] += lanes(cots)
    chunks = width // chunk
    units = pairs * chunks
    for q in range(chunks):
        cols = slice(q * chunk, (q + 1) * chunk)
        xp[:, cols] = jnp.dot(move[...], xs[:, cols], preferred_element_type=f32).astype(bf16)
    ones = jnp.ones((slab_rows, chunk), bf16)
    v1, a1, s1, v2, d2, a2, back, d1 = {}, {}, {}, {}, {}, {}, {}, {}

    def x_of(u):
        p, q = divmod(u, chunks)
        return xp[p * deep : (p + 1) * deep, q * chunk : (q + 1) * chunk]

    def first(u):
        v1[u] = jnp.dot(w1p[...], x_of(u), preferred_element_type=f32)

    def first_gelu(u):
        a, both, tail = gelu_parts(v1.pop(u))
        a1[u] = jnp.concatenate([a, ones], axis=0)
        s1[u] = both + tail.astype(f32)

    def second(u):
        v2[u] = jnp.dot(w2x[:, 0 : pair + slab_rows], a1[u], preferred_element_type=f32)

    def second_gelu(u):
        p, q = divmod(u, chunks)
        a2[u], both, tail = gelu_parts(v2.pop(u))
        cot = jnp.concatenate([
            jnp.broadcast_to(cot_ref[2 * p + k : 2 * p + k + 1, q * chunk : (q + 1) * chunk], (hidden, chunk))
            for k in range(2)], axis=0)
        d2[u] = (cot * (both + tail.astype(f32))).astype(bf16)

    def third(u):
        p, q = divmod(u, chunks)
        back[u] = jnp.dot(w2t[...], d2[u], preferred_element_type=f32)
        part = jnp.dot(rox[p], a2[u], preferred_element_type=f32)
        cols = slice(q * chunk, (q + 1) * chunk)
        if p == 0:
            pred_ref[:, cols] = part + rb_ref[0, 0]
        else:
            pred_ref[:, cols] += part
        if q == chunks - 1:
            mine = range(u - chunks + 1, u + 1)
            acc2[...] += lax.dot_general(
                jnp.concatenate([d2.pop(k) for k in mine], axis=1), jnp.concatenate([a1.pop(k) for k in mine], axis=1),
                NT, preferred_element_type=f32)

    def third_slope(u):
        d1[u] = (back.pop(u) * s1.pop(u)).astype(bf16)

    def fourth(u):
        if u % chunks == chunks - 1:
            mine = range(u - chunks + 1, u + 1)
            both = [jnp.concatenate([d1.pop(k), a2.pop(k)], axis=0) for k in mine]
            acc1[...] += lax.dot_general(
                jnp.concatenate([x_of(k) for k in mine], axis=1), jnp.concatenate(both, axis=1),
                NT, preferred_element_type=f32)

    for i in range(-3, units + 3):
        for stage, lag in ((first, 3), (second_gelu, 0), (second, 1), (first_gelu, 2), (third, -1), (third_slope, -2),
                           (fourth, -3)):
            if 0 <= i + lag < units:
                stage(i + lag)

    @pl.when(step == pl.num_programs(0) - 1)
    def _():
        total2 = acc2[...]
        g2 = total2[0:hidden, 0:hidden] + total2[hidden:pair, hidden:pair]
        ro = jnp.sum((iota((hidden, hidden), 0) == iota((hidden, hidden), 1)).astype(f32) * ro_ref[...].astype(f32),
                     axis=1, keepdims=True)
        g2 = 0.25 * ro * g2
        gb2 = 0.5 * ro * (total2[0:hidden, pair : pair + 1] + total2[hidden:pair, pair : pair + 1])
        flat = acc1[...]
        slot = iota((deep, pair), 0)
        side = iota((deep, pair), 1) // hidden
        keep = ((slot % 2 == side) & (slot < half)) | (slot == half)
        weights = jnp.where(keep, flat[:, 0:pair], 0.0)
        reads = jnp.where((slot % 2 == side) & (slot > half + 1), flat[:, pair : 2 * pair], 0.0)
        fold = (iota((pair, hidden), 0) % hidden == iota((pair, hidden), 1)).astype(f32)
        lane = iota((deep, hidden), 1)
        row = iota((deep, hidden), 0)
        place = (lane == jnp.where(row <= half, row // 2, -1)).astype(f32)
        place_r = ((lane == cin + 1) & (row > half + 1)).astype(f32)
        TN = (((0,), (0,)), ((), ()))
        exact = dict(precision=lax.Precision.HIGHEST, preferred_element_type=f32)
        up = jnp.dot(weights, fold, **exact)
        up_r = 0.5 * jnp.dot(reads, fold, **exact)
        g1 = lax.dot_general(up, place, TN, **exact) + lax.dot_general(up_r, place_r, TN, **exact)
        gb3 = jnp.sum(accc[...], keepdims=True)
        lane = iota((hidden, hidden), 1)
        right = jnp.where(lane == cin + 2, gb2, jnp.where(lane == cin + 3, gb3, g1))
        packed = jnp.concatenate([g2, right], axis=1)
        n, k, _ = grads_ref.shape
        for j in range(n):
            grads_ref[j] = packed[j * k : (j + 1) * k]


def mlp(demand, base, feats, cot, w1, b1, w2, b2, ro, rb, devices, width=1024, chunk=256):
    slab_rows, w = demand.shape
    hidden, cin = w1.shape
    pair = 2 * hidden
    depth = cin * slab_rows
    whole = lambda s: pl.BlockSpec(s, lambda i: tuple(0 for _ in s))
    cols = pl.BlockSpec((slab_rows, width), lambda i: (0, i))
    return pl.pallas_call(
        functools.partial(mlp_body, chunk),
        grid=(w // width,),
        in_specs=[
            cols, pl.BlockSpec((1, width), lambda i: (0, i)),
            pl.BlockSpec((cin - 1, slab_rows, width), lambda i: (0, 0, i)), cols,
            whole((hidden, cin)), whole((1, hidden)), whole((hidden, hidden)), whole((1, hidden)), whole((1, hidden)),
            pl.BlockSpec(memory_space=pltpu.SMEM),
        ],
        out_specs=[cols, whole((devices, hidden // devices, 2 * hidden))],
        out_shape=[
            jax.ShapeDtypeStruct((slab_rows, w), f32),
            jax.ShapeDtypeStruct((devices, hidden // devices, 2 * hidden), f32),
        ],
        scratch_shapes=[
            pltpu.VMEM((pair, 4 * cin), bf16),
            pltpu.VMEM((pair, pair + 128), bf16),
            pltpu.VMEM((pair, pair), bf16),
            pltpu.VMEM((slab_rows // 2, slab_rows, pair), bf16),
            pltpu.VMEM((2 * cin * slab_rows, depth + 3 * slab_rows), bf16),
            pltpu.VMEM((depth + 3 * slab_rows, width), bf16),
            pltpu.VMEM((2 * cin * slab_rows, width), bf16),
            pltpu.VMEM((4 * cin, 2 * pair), f32),
            pltpu.VMEM((pair, pair + slab_rows), f32),
            pltpu.VMEM((slab_rows, 128), f32),
        ],
        compiler_params=pltpu.CompilerParams(vmem_limit_bytes=40 * 1024 * 1024),
        name="mlp",
    )(demand, base, feats, cot, w1, b1[None, :], w2, b2[None, :], ro[None, :], rb[None, :])


def hail(n):
    me, group = lax.axis_index("canvas"), lax.axis_index("groups")
    barrier = pltpu.get_barrier_semaphore()

    def signal(k, carry):
        pl.semaphore_signal(
            barrier, inc=1, device_id=(group, lax.rem(me + k, n)), device_id_type=pl.DeviceIdType.MESH)
        return carry

    lax.fori_loop(1, n, signal, 0)


def all_here(n):
    pl.semaphore_wait(pltpu.get_barrier_semaphore(), n - 1)


def greet(n):
    hail(n)
    all_here(n)


def swap(n, source, target, send_sem, recv_sem):
    me, group = lax.axis_index("canvas"), lax.axis_index("groups")

    def copy(k, slot):
        peer = lax.rem(me + k, n)
        return pltpu.make_async_remote_copy(
            src_ref=source.at[peer], dst_ref=target.at[slot], send_sem=send_sem.at[k], recv_sem=recv_sem.at[k],
            device_id=(group, peer), device_id_type=pl.DeviceIdType.MESH)

    def start(k, carry):
        copy(k, me).start()
        return carry

    def arrive(k, carry):
        copy(k, lax.rem(me + n - k, n)).wait_recv()
        return carry

    lax.fori_loop(1, n, start, 0)
    target[pl.ds(me, 1)] = source[pl.ds(me, 1)]
    lax.fori_loop(1, n, arrive, 0)

    def finish():
        def left(k, carry):
            copy(k, me).wait_send()
            return carry

        lax.fori_loop(1, n, left, 0)

    return finish


def pack_items(n, slab_rows, w, slabs_ref, offsets_ref, left_ref, span_ref, pins_ref, send_ref):
    cap = send_ref.shape[2]
    one, two = slabs_ref[0:1, :], slabs_ref[1:2, :]
    off_one, off_two = offsets_ref[0:1, :], offsets_ref[1:2, :]
    first_is_low = one <= two
    low, high = jnp.minimum(one, two), jnp.maximum(one, two)
    low_row = jnp.where(first_is_low, off_one, off_two)
    high_row = jnp.where(first_is_low, off_two, off_one)
    left = left_ref[...]
    right = jnp.minimum(left + span_ref[...], w)
    wide = (right - left).astype(f32)
    tall = ((high - low) * slab_rows + high_row - low_row).astype(f32)
    weight = jnp.sqrt(pins_ref[...].astype(f32)) * (wide + tall) / (wide * tall)
    both = lambda x, y: jnp.concatenate([x, y], axis=1)
    slab = both(low, high)
    items = slab.shape[1]
    hot = jnp.where(iota((n, items), 0) == slab, 1.0, 0.0)
    hot_b = hot.astype(bf16)
    span = 256
    upper = (iota((span, span), 0) <= iota((span, span), 1)).astype(bf16)
    blocks = items // span
    before = ((iota((128, items), 1) // span) < iota((128, items), 0)).astype(bf16)
    starts = lax.dot_general(hot_b, before, NT, preferred_element_type=f32)
    counts = []
    for k in range(blocks):
        cols = slice(k * span, (k + 1) * span)
        inside = jnp.dot(hot_b[:, cols], upper, preferred_element_type=f32) + starts[:, k : k + 1]
        counts.append(jnp.sum(inside * hot[:, cols], axis=0, keepdims=True))
    rank = (jnp.concatenate(counts, axis=1) - 1.0).astype(i32)
    spot = jnp.where(iota((cap, items), 0) == rank, 1.0, 0.0).astype(bf16)
    amount = both(weight, -weight)
    coarse = amount.astype(bf16).astype(f32)
    row = both(low_row, high_row).astype(f32)
    start = both(left, left)
    end = both(right, right)
    start_low, end_low = start & 255, end & 255
    kind = iota((4 * n, items), 0) % 4
    mine = (iota((4 * n, items), 0) // 4) == slab

    def field(x0, x1, x2, x3):
        picked = jnp.where(kind == 0, x0, jnp.where(kind == 1, x1, jnp.where(kind == 2, x2, x3)))
        return jnp.where(mine, picked, 0.0).astype(bf16)

    big = field(coarse, row, (start - start_low).astype(f32), (end - end_low).astype(f32))
    small = field(amount - coarse, jnp.zeros_like(row), start_low.astype(f32), end_low.astype(f32))
    table = (lax.dot_general(big, spot, NT, preferred_element_type=f32)
             + lax.dot_general(small, spot, NT, preferred_element_type=f32))
    for d in range(n):
        send_ref[d] = table[4 * d : 4 * d + 4]


def slab(got_ref, local_ref, totals_ref, acc):
    n, _, cap = got_ref.shape
    slab_rows, w = local_ref.shape
    window = 256
    stride = window - 16
    tall = acc.shape[0]
    per = max(1, min(n, 2048 // cap))
    for c in range(n // per):
        def line(which):
            return jnp.concatenate([got_ref[c * per + j, which : which + 1, :] for j in range(per)], axis=1)

        value = line(0).astype(bf16).astype(f32)
        start = line(2)
        group = jnp.floor((start + 0.5) * (1.0 / stride))
        shift = group * stride
        first = (start - shift).astype(i32)
        last = (line(3) - shift).astype(i32)
        key = (group * slab_rows + line(1)).astype(i32)
        count = per * cap
        hot = jnp.where(iota((tall, count), 0) == key, 1.0, 0.0).astype(bf16)
        lane = iota((window, count), 0)
        fine = jnp.where((lane >= first) & (lane < last), value, 0.0).astype(bf16)
        update = lax.dot_general(hot, fine, NT, preferred_element_type=f32)
        if c == 0:
            acc[...] = update
        else:
            acc[...] += update
    tiles = [None] * (w // 128 + 4)
    for g in range(tall // slab_rows):
        at, turn = divmod(g * stride, 128)
        part = jnp.concatenate(
            [acc[g * slab_rows : (g + 1) * slab_rows, :], jnp.zeros((slab_rows, 128), f32)], axis=1)
        if turn:
            part = pltpu.roll(part, turn, 1)
        for k in range(3):
            piece = part[:, k * 128 : (k + 1) * 128]
            tiles[at + k] = piece if tiles[at + k] is None else tiles[at + k] + piece
    rows = iota((slab_rows, 128), 0)
    part = w // n
    for j in range(w // 128):
        t = tiles[j]
        step = 1
        while step < slab_rows:
            t = t + jnp.where(rows >= step, pltpu.roll(t, step, 0), 0.0)
            step *= 2
        local_ref[:, j * 128 : (j + 1) * 128] = t
    for d in range(n):
        totals_ref[d] = local_ref[slab_rows - 1 : slab_rows, d * part : (d + 1) * part]


def route_body(n, slabs_ref, offsets_ref, left_ref, span_ref, pins_ref, local_ref, base_ref,
               send, items, acc, totals, got, result, back, send_a, recv_a, send_b, recv_b, send_c, recv_c):
    hail(n)
    slab_rows, w = local_ref.shape
    pack_items(n, slab_rows, w, slabs_ref, offsets_ref, left_ref, span_ref, pins_ref, send)
    all_here(n)
    end_a = swap(n, send, items, send_a, recv_a)
    slab(items, local_ref, totals, acc)
    end_b = swap(n, totals, got, send_b, recv_b)
    running = jnp.zeros(got.shape[1:], f32)
    for d in range(n):
        result[d] = running
        running = running + got[d]
    end_c = swap(n, result, back, send_c, recv_c)
    part = got.shape[2]
    for d in range(n):
        base_ref[:, d * part : (d + 1) * part] = back[d]
    end_a()
    end_b()
    end_c()


def route(n, slabs, offsets, left, span, pins, slab_rows, w):
    cap = 4 * pins.shape[1] // n
    vmem = pl.BlockSpec(memory_space=pltpu.VMEM)
    part = pltpu.VMEM((n, 1, w // n), f32)
    groups = -(-w // 240)
    return pl.pallas_call(
        functools.partial(route_body, n),
        out_shape=[jax.ShapeDtypeStruct((slab_rows, w), f32), jax.ShapeDtypeStruct((1, w), f32)],
        in_specs=[vmem] * 5,
        out_specs=[vmem] * 2,
        scratch_shapes=[
            pltpu.VMEM((n, 4, cap), f32), pltpu.VMEM((n, 4, cap), f32), pltpu.VMEM((groups * slab_rows, 256), f32),
            part, part, part, part,
        ] + [pltpu.SemaphoreType.DMA((n,))] * 6,
        compiler_params=pltpu.CompilerParams(
            collective_id=0, has_side_effects=True, vmem_limit_bytes=48 * 1024 * 1024),
        name="route",
    )(slabs, offsets, left, span, pins)


def sum_body(n, grads_ref, total_ref, got, result, back, send_a, recv_a, send_b, recv_b):
    greet(n)
    end_a = swap(n, grads_ref, got, send_a, recv_a)
    total = got[0]
    for d in range(1, n):
        total = total + got[d]
    for d in range(n):
        result[d] = total
    end_b = swap(n, result, back, send_b, recv_b)
    k = got.shape[1]
    for d in range(n):
        total_ref[d * k : (d + 1) * k, :] = back[d]
    end_a()
    end_b()


def split_body(total_ref, g1_out, gb1_out, g2_out, gb2_out, gr_out, gb_out,
               g1_ref, gb1_ref, g2_ref, gb2_ref, gr_ref, gb_ref, out_sem):
    cin, hidden = g1_ref.shape
    g2_ref[...] = total_ref[:, 0:hidden]
    right = total_ref[:, hidden:]
    eye = iota((hidden, hidden), 0) == iota((hidden, hidden), 1)

    def row(lane):
        return jnp.sum(jnp.where(eye, right[:, lane : lane + 1], 0.0), axis=0, keepdims=True)

    g1_ref[...] = jnp.concatenate([row(c) for c in range(cin)], axis=0)
    gb1_ref[...] = row(cin).reshape(hidden)
    gr_ref[...] = row(cin + 1).reshape(hidden)
    gb2_ref[...] = row(cin + 2).reshape(hidden)
    gb_ref[...] = right[0:1, cin + 3 : cin + 4].reshape(1)
    pairs = ((g1_ref, g1_out), (gb1_ref, gb1_out), (g2_ref, g2_out), (gb2_ref, gb2_out), (gr_ref, gr_out),
             (gb_ref, gb_out))
    copies = [pltpu.make_async_copy(source, target, out_sem.at[i]) for i, (source, target) in enumerate(pairs)]
    for c in copies:
        c.start()
    for c in copies:
        c.wait()


def sum_all(grads, cin):
    n, k, _ = grads.shape
    hidden = n * k
    vmem = pl.BlockSpec(memory_space=pltpu.VMEM)
    line = (hidden,)
    shapes = ((cin, hidden), line, (hidden, hidden), line, line, (1,))
    total = linked(sum_body, n, grads, (hidden, 2 * hidden), 2, 1, "sum_all")
    return pl.pallas_call(
        split_body,
        out_shape=[jax.ShapeDtypeStruct(shape, f32) for shape in shapes],
        in_specs=[vmem],
        out_specs=[pl.BlockSpec(memory_space=pltpu.HBM)] * 6,
        scratch_shapes=[pltpu.VMEM(shape, f32) for shape in shapes] + [pltpu.SemaphoreType.DMA((6,))],
        name="split",
    )(total)


def linked(body, n, x, out_shape, phases, collective_id, name):
    vmem = pl.BlockSpec(memory_space=pltpu.VMEM)
    extra = [pltpu.VMEM(x.shape, f32)] * 3 if phases == 2 else []
    return pl.pallas_call(
        functools.partial(body, n),
        out_shape=jax.ShapeDtypeStruct(out_shape, f32),
        in_specs=[vmem],
        out_specs=vmem,
        scratch_shapes=extra + [pltpu.SemaphoreType.DMA((n,))] * (2 * phases),
        compiler_params=pltpu.CompilerParams(collective_id=collective_id, has_side_effects=True),
        name=name,
    )(x)


def per_device(
    net_slabs,
    row_offsets,
    left_column,
    column_span,
    pin_counts,
    tile_features,
    cotangent,
    first_weight,
    first_bias,
    second_weight,
    second_bias,
    readout_weight,
    readout_bias,
):
    devices = lax.axis_size("canvas")
    slab_rows = tile_features.shape[1]
    canvas_width = tile_features.shape[2]
    local, base = route(
        devices, net_slabs.T, row_offsets.T, left_column[None, :], column_span[None, :], pin_counts[None, :],
        slab_rows, canvas_width)
    prediction, grads = mlp(
        local, base, tile_features, cotangent, first_weight, first_bias, second_weight, second_bias,
        readout_weight, readout_bias, devices)
    g1, gb1, g2, gb2, gr, gb = sum_all(grads, first_weight.shape[1])
    return (prediction, g1.T, gb1, g2, gb2, gr, gb)


def solution(mesh):
    in_specs = (
        P(("groups", "canvas"), None),
        P(("groups", "canvas"), None),
        P(("groups", "canvas")),
        P(("groups", "canvas")),
        P(("groups", "canvas")),
        P(None, ("groups", "canvas"), None),
        P(("groups", "canvas"), None),
        P(),
        P(),
        P(),
        P(),
        P(),
        P(),
    )
    out_specs = (
        P(("groups", "canvas"), None),
        P("groups", None),
        P("groups"),
        P("groups", None),
        P("groups"),
        P("groups"),
        P("groups"),
    )
    return jax.shard_map(
        per_device, mesh=mesh, in_specs=in_specs, out_specs=out_specs, check_vma=False
    )
```

```python
import functools
import jax
import jax.numpy as jnp
from jax import lax
from jax.experimental import pallas as pl
from jax.experimental.pallas import tpu as pltpu
from jax.sharding import PartitionSpec as P

root_half = 0.7071067811865476
log2_two_over_root_pi = 0.17425071
log2e = 1.4426950408889634
vmem_most = 60 * 1024 * 1024
f32 = jnp.float32
bf16 = jnp.bfloat16
i32 = jnp.int32
NT = (((1,), (1,)), ((), ()))


def iota(shape, dim):
    return lax.broadcasted_iota(i32, shape, dim)


def lanes(a):
    return sum(a[:, k * 128 : (k + 1) * 128] for k in range(a.shape[1] // 128))


def gelu_parts(v):
    w = v * root_half
    both = 1.0 + lax.erf(w)
    w = w.astype(bf16)
    tail = w * jnp.exp2((w * w) * bf16(-log2e) + bf16(log2_two_over_root_pi))
    return (v * both).astype(bf16), both, tail


def split_column(b):
    high = b.astype(bf16).astype(f32)
    return high, b - high


def mlp_body(chunk, demand_ref, base_ref, feat_ref, cot_ref, w1_ref, b1_ref, w2_ref, b2_ref, ro_ref, rb_ref,
             pred_ref, grads_ref,
             w1p, w2x, w2t, rox, move, xs, xp, acc1, acc2, accc):
    step = pl.program_id(0)
    slab_rows, width = demand_ref.shape
    cin, hidden = w1_ref.shape
    pair = 2 * hidden
    pairs = slab_rows // 2
    depth = cin * slab_rows
    deep = 4 * cin
    half = 2 * cin
    reach = xs.shape[0]

    @pl.when(step == 0)
    def _():
        pick = (iota((pair, hidden), 0) % hidden == iota((pair, hidden), 1)).astype(bf16)
        pick_f = pick.astype(f32)
        spread = (iota((cin, deep), 1) // 2 == iota((cin, deep), 0)).astype(bf16)
        tall = lax.dot_general(pick, w1_ref[...], NT, preferred_element_type=f32).astype(bf16)
        wide = jnp.dot(tall, spread, preferred_element_type=f32)
        high, low = split_column(jnp.sum(pick_f * b1_ref[...], axis=1, keepdims=True))
        lane = iota((pair, deep), 1)
        keep = iota((pair, deep), 0) // hidden == lane % 2
        w1p[...] = jnp.where(
            lane == half, high, jnp.where(lane == half + 1, low, jnp.where(keep, wide, 0.0))).astype(bf16)
        same = iota((pair, pair), 0) // hidden == iota((pair, pair), 1) // hidden
        down = jnp.dot(pick, w2_ref[...], preferred_element_type=f32).astype(bf16)
        full = lax.dot_general(down, pick, NT, preferred_element_type=f32)
        w2x[:, 0:pair] = jnp.where(same, 0.5 * full, 0.0).astype(bf16)
        high, low = split_column(jnp.sum(pick_f * b2_ref[...], axis=1, keepdims=True))
        lane = iota((pair, 128), 1)
        w2x[:, pair : pair + 128] = jnp.where(lane == 0, high, jnp.where(lane == 1, low, 0.0)).astype(bf16)
        flip = lax.dot_general(pick, w2_ref[...], NT, preferred_element_type=f32).astype(bf16)
        full_t = lax.dot_general(flip, pick, NT, preferred_element_type=f32)
        ro_wide = lax.dot_general(ro_ref[...], pick, NT, preferred_element_type=f32)
        w2t[...] = jnp.where(same, 0.25 * full_t * ro_wide, 0.0).astype(bf16)
        ro_rows = 0.5 * jnp.broadcast_to(ro_wide, (slab_rows, pair))
        for p in range(pairs):
            here = iota((slab_rows, pair), 0) == iota((slab_rows, pair), 1) // hidden + 2 * p
            rox[p] = jnp.where(here, ro_rows, 0.0).astype(bf16)
        line = iota((pairs * deep, reach), 0)
        slot = line % deep
        row = 2 * (line // deep) + slot % 2
        source = jnp.where(slot < half, (slot // 2) * slab_rows + row,
                           jnp.where(slot < half + 2, depth + 2 * slab_rows,
                                     jnp.where(slot < half + 6, depth + (slot // 2 - cin - 1) * slab_rows + row, -1)))
        move[...] = (iota((pairs * deep, reach), 1) == source).astype(bf16)
        acc1[...] = jnp.zeros_like(acc1)
        acc2[...] = jnp.zeros_like(acc2)
        accc[...] = jnp.zeros_like(accc)
        xs[depth + 2 * slab_rows : reach, :] = jnp.ones((reach - depth - 2 * slab_rows, width), bf16)

    cots = cot_ref[...]
    cot_high = cots.astype(bf16)
    xs[0:slab_rows, :] = jnp.log(1.0 + (demand_ref[...] + base_ref[...])).astype(bf16)
    xs[slab_rows:depth, :] = feat_ref[...].reshape((cin - 1) * slab_rows, width)
    xs[depth : depth + slab_rows, :] = cot_high
    xs[depth + slab_rows : depth + 2 * slab_rows, :] = (cots - cot_high.astype(f32)).astype(bf16)
    accc[...] += lanes(cots)
    chunks = width // chunk
    units = pairs * chunks
    for q in range(chunks):
        cols = slice(q * chunk, (q + 1) * chunk)
        xp[:, cols] = jnp.dot(move[...], xs[:, cols], preferred_element_type=f32).astype(bf16)
    ones = jnp.ones((slab_rows, chunk), bf16)
    v1, a1, s1, v2, d2, a2, back, d1 = {}, {}, {}, {}, {}, {}, {}, {}

    def x_of(u):
        p, q = divmod(u, chunks)
        return xp[p * deep : (p + 1) * deep, q * chunk : (q + 1) * chunk]

    def first(u):
        v1[u] = jnp.dot(w1p[...], x_of(u), preferred_element_type=f32)

    def first_gelu(u):
        a, both, tail = gelu_parts(v1.pop(u))
        a1[u] = jnp.concatenate([a, ones], axis=0)
        s1[u] = both + tail.astype(f32)

    def second(u):
        v2[u] = jnp.dot(w2x[:, 0 : pair + slab_rows], a1[u], preferred_element_type=f32)

    def second_gelu(u):
        p, q = divmod(u, chunks)
        a2[u], both, tail = gelu_parts(v2.pop(u))
        cot = jnp.concatenate([
            jnp.broadcast_to(cot_ref[2 * p + k : 2 * p + k + 1, q * chunk : (q + 1) * chunk], (hidden, chunk))
            for k in range(2)], axis=0)
        d2[u] = (cot * (both + tail.astype(f32))).astype(bf16)

    def third(u):
        p, q = divmod(u, chunks)
        back[u] = jnp.dot(w2t[...], d2[u], preferred_element_type=f32)
        part = jnp.dot(rox[p], a2[u], preferred_element_type=f32)
        cols = slice(q * chunk, (q + 1) * chunk)
        if p == 0:
            pred_ref[:, cols] = part + rb_ref[0, 0]
        else:
            pred_ref[:, cols] += part
        if q == chunks - 1:
            mine = range(u - chunks + 1, u + 1)
            acc2[...] += lax.dot_general(
                jnp.concatenate([d2.pop(k) for k in mine], axis=1), jnp.concatenate([a1.pop(k) for k in mine], axis=1),
                NT, preferred_element_type=f32)

    def third_slope(u):
        d1[u] = (back.pop(u) * s1.pop(u)).astype(bf16)

    def fourth(u):
        if u % chunks == chunks - 1:
            mine = range(u - chunks + 1, u + 1)
            both = [jnp.concatenate([d1.pop(k), a2.pop(k)], axis=0) for k in mine]
            acc1[...] += lax.dot_general(
                jnp.concatenate([x_of(k) for k in mine], axis=1), jnp.concatenate(both, axis=1),
                NT, preferred_element_type=f32)

    for i in range(-3, units + 3):
        for stage, lag in ((first, 3), (second_gelu, 0), (second, 1), (first_gelu, 2), (third, -1), (third_slope, -2),
                           (fourth, -3)):
            if 0 <= i + lag < units:
                stage(i + lag)

    @pl.when(step == pl.num_programs(0) - 1)
    def _():
        total2 = acc2[...]
        g2 = total2[0:hidden, 0:hidden] + total2[hidden:pair, hidden:pair]
        ro = jnp.sum((iota((hidden, hidden), 0) == iota((hidden, hidden), 1)).astype(f32) * ro_ref[...].astype(f32),
                     axis=1, keepdims=True)
        g2 = 0.25 * ro * g2
        bias = 0.5 * ro * (total2[0:hidden, pair : pair + 1] + total2[hidden:pair, pair : pair + 1])
        eye = iota((hidden, hidden), 0) == iota((hidden, hidden), 1)
        gb2 = jnp.sum(jnp.where(eye, bias, 0.0), axis=0, keepdims=True)
        flat = acc1[...]
        slot = iota((deep, pair), 0)
        side = iota((deep, pair), 1) // hidden
        keep = ((slot % 2 == side) & (slot < half)) | (slot == half)
        weights = jnp.where(keep, flat[:, 0:pair], 0.0)
        reads = jnp.where((slot % 2 == side) & (slot > half + 1), flat[:, pair : 2 * pair], 0.0)
        fold = (iota((pair, hidden), 0) % hidden == iota((pair, hidden), 1)).astype(f32)
        exact = dict(precision=lax.Precision.HIGHEST, preferred_element_type=f32)
        up = jnp.dot(weights, fold, **exact)
        up_r = jnp.dot(reads, fold, **exact)
        joined = jnp.where(iota((cin, deep), 1) // 2 == iota((cin, deep), 0), 1.0, 0.0)
        g1 = jnp.dot(joined, up, **exact)
        gb1 = up[half : half + 1]
        gr = 0.5 * jnp.sum(up_r, axis=0, keepdims=True)
        gb3 = jnp.broadcast_to(jnp.sum(accc[...], keepdims=True), (1, hidden))
        lines = jnp.concatenate([gb1, gr, gb2, gb3, jnp.zeros((cin - 4, hidden), f32)], axis=0)
        body = hidden // 2
        grads_ref[0:body] = jnp.concatenate([g2[0:body], g2[body:hidden]], axis=1)
        grads_ref[body : body + cin] = jnp.concatenate([g1, lines], axis=1)
        rest = grads_ref.shape[0] - body - cin
        grads_ref[body + cin :] = jnp.zeros((rest, 2 * hidden), f32)


def sum_rows(hidden):
    return (hidden // 2 + 8 + 15) // 16 * 16


def mlp(demand, base, feats, cot, w1, b1, w2, b2, ro, rb, width=1024, chunk=256):
    slab_rows, w = demand.shape
    hidden, cin = w1.shape
    packed = (sum_rows(hidden), 2 * hidden)
    pair = 2 * hidden
    depth = cin * slab_rows
    whole = lambda s: pl.BlockSpec(s, lambda i: tuple(0 for _ in s))
    cols = pl.BlockSpec((slab_rows, width), lambda i: (0, i))
    return pl.pallas_call(
        functools.partial(mlp_body, chunk),
        grid=(w // width,),
        in_specs=[
            cols, pl.BlockSpec((1, width), lambda i: (0, i)),
            pl.BlockSpec((cin - 1, slab_rows, width), lambda i: (0, 0, i)), cols,
            whole((cin, hidden)), whole((1, hidden)), whole((hidden, hidden)), whole((1, hidden)), whole((1, hidden)),
            pl.BlockSpec(memory_space=pltpu.SMEM),
        ],
        out_specs=[cols, whole(packed)],
        out_shape=[
            jax.ShapeDtypeStruct((slab_rows, w), f32),
            jax.ShapeDtypeStruct(packed, f32),
        ],
        scratch_shapes=[
            pltpu.VMEM((pair, 4 * cin), bf16),
            pltpu.VMEM((pair, pair + 128), bf16),
            pltpu.VMEM((pair, pair), bf16),
            pltpu.VMEM((slab_rows // 2, slab_rows, pair), bf16),
            pltpu.VMEM((2 * cin * slab_rows, depth + 3 * slab_rows), bf16),
            pltpu.VMEM((depth + 3 * slab_rows, width), bf16),
            pltpu.VMEM((2 * cin * slab_rows, width), bf16),
            pltpu.VMEM((4 * cin, 2 * pair), f32),
            pltpu.VMEM((pair, pair + slab_rows), f32),
            pltpu.VMEM((slab_rows, 128), f32),
        ],
        compiler_params=pltpu.CompilerParams(vmem_limit_bytes=vmem_most),
        name="mlp",
    )(demand, base, feats, cot, w1.T, b1[None, :], w2, b2[None, :], ro[None, :], rb[None, :])


def hail(n):
    me, group = lax.axis_index("canvas"), lax.axis_index("groups")
    barrier = pltpu.get_barrier_semaphore()

    def signal(k, carry):
        pl.semaphore_signal(
            barrier, inc=1, device_id=(group, lax.rem(me + k, n)), device_id_type=pl.DeviceIdType.MESH)
        return carry

    lax.fori_loop(1, n, signal, 0)


def all_here(n):
    pl.semaphore_wait(pltpu.get_barrier_semaphore(), n - 1)


def greet(n):
    hail(n)
    all_here(n)


def swap(n, source, target, send_sem, recv_sem):
    me, group = lax.axis_index("canvas"), lax.axis_index("groups")

    def copy(k, slot):
        peer = lax.rem(me + k, n)
        return pltpu.make_async_remote_copy(
            src_ref=source.at[peer], dst_ref=target.at[slot], send_sem=send_sem.at[k], recv_sem=recv_sem.at[k],
            device_id=(group, peer), device_id_type=pl.DeviceIdType.MESH)

    def start(k, carry):
        copy(k, me).start()
        return carry

    def arrive(k, carry):
        copy(k, lax.rem(me + n - k, n)).wait_recv()
        return carry

    lax.fori_loop(1, n, start, 0)
    target[pl.ds(me, 1)] = source[pl.ds(me, 1)]
    lax.fori_loop(1, n, arrive, 0)

    def finish():
        def left(k, carry):
            copy(k, me).wait_send()
            return carry

        lax.fori_loop(1, n, left, 0)

    return finish


def pack_items(n, slab_rows, w, slabs_ref, offsets_ref, left_ref, span_ref, pins_ref, send_ref):
    cap = send_ref.shape[2]
    one, two = slabs_ref[0:1, :], slabs_ref[1:2, :]
    off_one, off_two = offsets_ref[0:1, :], offsets_ref[1:2, :]
    first_is_low = one <= two
    low, high = jnp.minimum(one, two), jnp.maximum(one, two)
    low_row = jnp.where(first_is_low, off_one, off_two)
    high_row = jnp.where(first_is_low, off_two, off_one)
    left = left_ref[...]
    right = jnp.minimum(left + span_ref[...], w)
    wide = (right - left).astype(f32)
    tall = ((high - low) * slab_rows + high_row - low_row).astype(f32)
    weight = jnp.sqrt(pins_ref[...].astype(f32)) * (wide + tall) / (wide * tall)
    both = lambda x, y: jnp.concatenate([x, y], axis=1)
    slab = both(low, high)
    items = slab.shape[1]
    hot = jnp.where(iota((n, items), 0) == slab, 1.0, 0.0)
    hot_b = hot.astype(bf16)
    span = 256
    upper = (iota((span, span), 0) <= iota((span, span), 1)).astype(bf16)
    blocks = items // span
    before = ((iota((128, items), 1) // span) < iota((128, items), 0)).astype(bf16)
    starts = lax.dot_general(hot_b, before, NT, preferred_element_type=f32)
    counts = []
    for k in range(blocks):
        cols = slice(k * span, (k + 1) * span)
        inside = jnp.dot(hot_b[:, cols], upper, preferred_element_type=f32) + starts[:, k : k + 1]
        counts.append(jnp.sum(inside * hot[:, cols], axis=0, keepdims=True))
    rank = (jnp.concatenate(counts, axis=1) - 1.0).astype(i32)
    spot = jnp.where(iota((cap, items), 0) == rank, 1.0, 0.0).astype(bf16)
    amount = both(weight, -weight)
    coarse = amount.astype(bf16).astype(f32)
    row = both(low_row, high_row).astype(f32)
    start = both(left, left)
    end = both(right, right)
    start_low, end_low = start & 255, end & 255
    kind = iota((4 * n, items), 0) % 4
    mine = (iota((4 * n, items), 0) // 4) == slab

    def field(x0, x1, x2, x3):
        picked = jnp.where(kind == 0, x0, jnp.where(kind == 1, x1, jnp.where(kind == 2, x2, x3)))
        return jnp.where(mine, picked, 0.0).astype(bf16)

    big = field(coarse, row, (start - start_low).astype(f32), (end - end_low).astype(f32))
    small = field(amount - coarse, jnp.zeros_like(row), start_low.astype(f32), end_low.astype(f32))
    table = (lax.dot_general(big, spot, NT, preferred_element_type=f32)
             + lax.dot_general(small, spot, NT, preferred_element_type=f32))
    for d in range(n):
        send_ref[d] = table[4 * d : 4 * d + 4]


def slab(got_ref, local_ref, totals_ref, acc):
    n, _, cap = got_ref.shape
    slab_rows, w = local_ref.shape
    window = 256
    stride = window - 16
    tall = acc.shape[0]
    per = max(1, min(n, 2048 // cap))
    for c in range(n // per):
        def line(which):
            return jnp.concatenate([got_ref[c * per + j, which : which + 1, :] for j in range(per)], axis=1)

        value = line(0).astype(bf16).astype(f32)
        start = line(2)
        group = jnp.floor((start + 0.5) * (1.0 / stride))
        shift = group * stride
        first = (start - shift).astype(i32)
        last = (line(3) - shift).astype(i32)
        key = (group * slab_rows + line(1)).astype(i32)
        count = per * cap
        hot = jnp.where(iota((tall, count), 0) == key, 1.0, 0.0).astype(bf16)
        lane = iota((window, count), 0)
        fine = jnp.where((lane >= first) & (lane < last), value, 0.0).astype(bf16)
        update = lax.dot_general(hot, fine, NT, preferred_element_type=f32)
        if c == 0:
            acc[...] = update
        else:
            acc[...] += update
    tiles = [None] * (w // 128 + 4)
    for g in range(tall // slab_rows):
        at, turn = divmod(g * stride, 128)
        part = jnp.concatenate(
            [acc[g * slab_rows : (g + 1) * slab_rows, :], jnp.zeros((slab_rows, 128), f32)], axis=1)
        if turn:
            part = pltpu.roll(part, turn, 1)
        for k in range(3):
            piece = part[:, k * 128 : (k + 1) * 128]
            tiles[at + k] = piece if tiles[at + k] is None else tiles[at + k] + piece
    rows = iota((slab_rows, 128), 0)
    part = w // n
    for j in range(w // 128):
        t = tiles[j]
        step = 1
        while step < slab_rows:
            t = t + jnp.where(rows >= step, pltpu.roll(t, step, 0), 0.0)
            step *= 2
        local_ref[:, j * 128 : (j + 1) * 128] = t
    for d in range(n):
        totals_ref[d] = local_ref[slab_rows - 1 : slab_rows, d * part : (d + 1) * part]


def route_body(n, slabs_ref, offsets_ref, left_ref, span_ref, pins_ref, local_ref, base_ref,
               send, items, acc, totals, got, result, back, send_a, recv_a, send_b, recv_b, send_c, recv_c):
    hail(n)
    slab_rows, w = local_ref.shape
    pack_items(n, slab_rows, w, slabs_ref, offsets_ref, left_ref, span_ref, pins_ref, send)
    all_here(n)
    end_a = swap(n, send, items, send_a, recv_a)
    slab(items, local_ref, totals, acc)
    end_b = swap(n, totals, got, send_b, recv_b)
    running = jnp.zeros(got.shape[1:], f32)
    for d in range(n):
        result[d] = running
        running = running + got[d]
    end_c = swap(n, result, back, send_c, recv_c)
    part = got.shape[2]
    for d in range(n):
        base_ref[:, d * part : (d + 1) * part] = back[d]
    end_a()
    end_b()
    end_c()


def route(n, slabs, offsets, left, span, pins, slab_rows, w):
    cap = 4 * pins.shape[1] // n
    vmem = pl.BlockSpec(memory_space=pltpu.VMEM)
    part = pltpu.VMEM((n, 1, w // n), f32)
    groups = -(-w // 240)
    return pl.pallas_call(
        functools.partial(route_body, n),
        out_shape=[jax.ShapeDtypeStruct((slab_rows, w), f32), jax.ShapeDtypeStruct((1, w), f32)],
        in_specs=[vmem] * 5,
        out_specs=[vmem] * 2,
        scratch_shapes=[
            pltpu.VMEM((n, 4, cap), f32), pltpu.VMEM((n, 4, cap), f32), pltpu.VMEM((groups * slab_rows, 256), f32),
            part, part, part, part,
        ] + [pltpu.SemaphoreType.DMA((n,))] * 6,
        compiler_params=pltpu.CompilerParams(
            collective_id=0, has_side_effects=True, vmem_limit_bytes=vmem_most),
        name="route",
    )(slabs, offsets, left, span, pins)


def sum_body(n, grads_ref, total_ref, sibling, mine, halves, full, send_sem, recv_sem, pair_send, pair_recv):
    me, group = lax.axis_index("canvas"), lax.axis_index("groups")
    core = lax.rem(me, 2)
    chip = me // 2
    other = me + 1 - 2 * core
    chips = n // 2
    rows = halves.shape[1]
    barrier = pltpu.get_barrier_semaphore()

    def friend(k):
        return 2 * lax.rem(chip + k, chips) + core

    def signal(k, carry):
        pl.semaphore_signal(barrier, inc=1, device_id=(group, friend(k)), device_id_type=pl.DeviceIdType.MESH)
        return carry

    pl.semaphore_signal(barrier, inc=1, device_id=(group, other), device_id_type=pl.DeviceIdType.MESH)
    lax.fori_loop(1, chips, signal, 0)
    pl.semaphore_wait(barrier, chips)

    def hand(source, target, which):
        return pltpu.make_async_remote_copy(
            src_ref=source, dst_ref=target, send_sem=pair_send.at[which], recv_sem=pair_recv.at[which],
            device_id=(group, other), device_id_type=pl.DeviceIdType.MESH)

    first = hand(grads_ref, sibling, 0)
    first.start()
    first.wait_recv()
    mine[...] = grads_ref[...] + sibling[...]
    part = pl.ds(pl.multiple_of(core * rows, 8), rows)

    def copy(k, slot):
        return pltpu.make_async_remote_copy(
            src_ref=mine.at[part], dst_ref=halves.at[slot], send_sem=send_sem.at[k], recv_sem=recv_sem.at[k],
            device_id=(group, friend(k)), device_id_type=pl.DeviceIdType.MESH)

    def start(k, carry):
        copy(k, chip).start()
        return carry

    def arrive(k, carry):
        copy(k, lax.rem(chip + chips - k, chips)).wait_recv()
        return carry

    lax.fori_loop(1, chips, start, 0)
    halves[pl.ds(chip, 1)] = mine[part][None]
    lax.fori_loop(1, chips, arrive, 0)
    total = halves[0]
    for d in range(1, chips):
        total = total + halves[d]
    full[part] = total
    last = hand(full.at[part], full.at[part], 1)
    last.start()

    def left(k, carry):
        copy(k, chip).wait_send()
        return carry

    lax.fori_loop(1, chips, left, 0)
    first.wait_send()
    last.wait()
    total_ref[...] = full[...]


def split_body(cin, total_ref, g1_out, gb1_out, g2_out, gb2_out, gr_out, gb_out,
               g1_ref, gb1_ref, g2_ref, gb2_ref, gr_ref, gb_ref, out_sem):
    hidden = g1_ref.shape[1]
    body = hidden // 2
    g2_ref[0:body] = total_ref[0:body, 0:hidden]
    g2_ref[body:hidden] = total_ref[0:body, hidden:]
    g1_ref[...] = total_ref[body : body + cin, 0:hidden]
    for k, target in enumerate((gb1_ref, gr_ref, gb2_ref)):
        target[...] = total_ref[body + k : body + k + 1, hidden:].reshape(hidden)
    gb_ref[...] = total_ref[body + 3 : body + 4, hidden : hidden + 1].reshape(1)
    pairs = ((g1_ref, g1_out), (gb1_ref, gb1_out), (g2_ref, g2_out), (gb2_ref, gb2_out), (gr_ref, gr_out),
             (gb_ref, gb_out))
    copies = [pltpu.make_async_copy(source, target, out_sem.at[i]) for i, (source, target) in enumerate(pairs)]
    for c in copies:
        c.start()
    for c in copies:
        c.wait()


def sum_all(grads, n, shape):
    hidden, cin = shape
    vmem = pl.BlockSpec(memory_space=pltpu.VMEM)
    line = (hidden,)
    shapes = ((cin, hidden), line, (hidden, hidden), line, line, (1,))
    whole = pltpu.VMEM(grads.shape, f32)
    total = pl.pallas_call(
        functools.partial(sum_body, n),
        out_shape=jax.ShapeDtypeStruct(grads.shape, f32),
        in_specs=[vmem],
        out_specs=vmem,
        scratch_shapes=[whole, whole, pltpu.VMEM((n // 2, grads.shape[0] // 2, grads.shape[1]), f32), whole]
        + [pltpu.SemaphoreType.DMA((n // 2,))] * 2 + [pltpu.SemaphoreType.DMA((2,))] * 2,
        compiler_params=pltpu.CompilerParams(collective_id=1, has_side_effects=True),
        name="sum_all",
    )(grads)
    return pl.pallas_call(
        functools.partial(split_body, cin),
        out_shape=[jax.ShapeDtypeStruct(shape, f32) for shape in shapes],
        in_specs=[vmem],
        out_specs=[pl.BlockSpec(memory_space=pltpu.HBM)] * 6,
        scratch_shapes=[pltpu.VMEM(shape, f32) for shape in shapes] + [pltpu.SemaphoreType.DMA((6,))],
        name="split",
    )(total)


def per_device(
    net_slabs,
    row_offsets,
    left_column,
    column_span,
    pin_counts,
    tile_features,
    cotangent,
    first_weight,
    first_bias,
    second_weight,
    second_bias,
    readout_weight,
    readout_bias,
):
    devices = lax.axis_size("canvas")
    slab_rows = tile_features.shape[1]
    canvas_width = tile_features.shape[2]
    local, base = route(
        devices, net_slabs.T, row_offsets.T, left_column[None, :], column_span[None, :], pin_counts[None, :],
        slab_rows, canvas_width)
    prediction, grads = mlp(
        local, base, tile_features, cotangent, first_weight, first_bias, second_weight, second_bias,
        readout_weight, readout_bias)
    g1, gb1, g2, gb2, gr, gb = sum_all(grads, devices, first_weight.shape)
    return (prediction, g1.T, gb1, g2, gb2, gr, gb)


def solution(mesh):
    in_specs = (
        P(("groups", "canvas"), None),
        P(("groups", "canvas"), None),
        P(("groups", "canvas")),
        P(("groups", "canvas")),
        P(("groups", "canvas")),
        P(None, ("groups", "canvas"), None),
        P(("groups", "canvas"), None),
        P(),
        P(),
        P(),
        P(),
        P(),
        P(),
    )
    out_specs = (
        P(("groups", "canvas"), None),
        P("groups", None),
        P("groups"),
        P("groups", None),
        P("groups"),
        P("groups"),
        P("groups"),
    )
    return jax.shard_map(
        per_device, mesh=mesh, in_specs=in_specs, out_specs=out_specs, check_vma=False
    )
```

```python
import functools
import jax
import jax.numpy as jnp
from jax import lax
from jax.experimental import pallas as pl
from jax.experimental.pallas import tpu as pltpu
from jax.sharding import PartitionSpec as P

root_half = 0.7071067811865476
log2_two_over_root_pi = 0.17425071
log2e = 1.4426950408889634
vmem_most = 60 * 1024 * 1024
f32 = jnp.float32
bf16 = jnp.bfloat16
i32 = jnp.int32
NT = (((1,), (1,)), ((), ()))


def iota(shape, dim):
    return lax.broadcasted_iota(i32, shape, dim)


def lanes(a):
    return sum(a[:, k * 128 : (k + 1) * 128] for k in range(a.shape[1] // 128))


def gelu_parts(v):
    w = v * root_half
    both = 1.0 + lax.erf(w)
    w = w.astype(bf16)
    tail = w * jnp.exp2((w * w) * bf16(-log2e) + bf16(log2_two_over_root_pi))
    return (v * both).astype(bf16), both, tail


def split_column(b):
    high = b.astype(bf16).astype(f32)
    return high, b - high


def mlp_body(chunk, demand_ref, base_ref, feat_ref, cot_ref, w1_ref, b1_ref, w2_ref, b2_ref, ro_ref, rb_ref,
             pred_ref, grads_ref,
             w1p, w2x, w2t, rox, move, xs, xp, acc1, acc2, accc):
    step = pl.program_id(0)
    slab_rows, width = demand_ref.shape
    cin, hidden = w1_ref.shape
    pair = 2 * hidden
    pairs = slab_rows // 2
    depth = cin * slab_rows
    deep = 4 * cin
    half = 2 * cin
    reach = xs.shape[0]

    @pl.when(step == 0)
    def _():
        pick = (iota((pair, hidden), 0) % hidden == iota((pair, hidden), 1)).astype(bf16)
        pick_f = pick.astype(f32)
        spread = (iota((cin, deep), 1) // 2 == iota((cin, deep), 0)).astype(bf16)
        tall = lax.dot_general(pick, w1_ref[...], NT, preferred_element_type=f32).astype(bf16)
        wide = jnp.dot(tall, spread, preferred_element_type=f32)
        high, low = split_column(jnp.sum(pick_f * b1_ref[...], axis=1, keepdims=True))
        lane = iota((pair, deep), 1)
        keep = iota((pair, deep), 0) // hidden == lane % 2
        w1p[...] = jnp.where(
            lane == half, high, jnp.where(lane == half + 1, low, jnp.where(keep, wide, 0.0))).astype(bf16)
        same = iota((pair, pair), 0) // hidden == iota((pair, pair), 1) // hidden
        down = jnp.dot(pick, w2_ref[...], preferred_element_type=f32).astype(bf16)
        full = lax.dot_general(down, pick, NT, preferred_element_type=f32)
        w2x[:, 0:pair] = jnp.where(same, 0.5 * full, 0.0).astype(bf16)
        high, low = split_column(jnp.sum(pick_f * b2_ref[...], axis=1, keepdims=True))
        lane = iota((pair, 128), 1)
        w2x[:, pair : pair + 128] = jnp.where(lane == 0, high, jnp.where(lane == 1, low, 0.0)).astype(bf16)
        flip = lax.dot_general(pick, w2_ref[...], NT, preferred_element_type=f32).astype(bf16)
        full_t = lax.dot_general(flip, pick, NT, preferred_element_type=f32)
        ro_wide = lax.dot_general(ro_ref[...], pick, NT, preferred_element_type=f32)
        w2t[...] = jnp.where(same, 0.25 * full_t * ro_wide, 0.0).astype(bf16)
        ro_rows = 0.5 * jnp.broadcast_to(ro_wide, (slab_rows, pair))
        for p in range(pairs):
            here = iota((slab_rows, pair), 0) == iota((slab_rows, pair), 1) // hidden + 2 * p
            rox[p] = jnp.where(here, ro_rows, 0.0).astype(bf16)
        line = iota((pairs * deep, reach), 0)
        slot = line % deep
        row = 2 * (line // deep) + slot % 2
        source = jnp.where(slot < half, (slot // 2) * slab_rows + row,
                           jnp.where(slot < half + 2, depth + 2 * slab_rows,
                                     jnp.where(slot < half + 6, depth + (slot // 2 - cin - 1) * slab_rows + row, -1)))
        move[...] = (iota((pairs * deep, reach), 1) == source).astype(bf16)
        acc1[...] = jnp.zeros_like(acc1)
        acc2[...] = jnp.zeros_like(acc2)
        accc[...] = jnp.zeros_like(accc)
        xs[depth + 2 * slab_rows : reach, :] = jnp.ones((reach - depth - 2 * slab_rows, width), bf16)

    chunks = width // chunk
    units = pairs * chunks
    joint = 4

    def prepare(q):
        cols = slice(q * chunk, (q + 1) * chunk)
        cot = cot_ref[:, cols]
        high = cot.astype(bf16)
        xs[0:slab_rows, cols] = jnp.log(1.0 + (demand_ref[:, cols] + base_ref[:, cols])).astype(bf16)
        xs[slab_rows:depth, cols] = feat_ref[:, :, cols].reshape((cin - 1) * slab_rows, chunk)
        xs[depth : depth + slab_rows, cols] = high
        xs[depth + slab_rows : depth + 2 * slab_rows, cols] = (cot - high.astype(f32)).astype(bf16)
        accc[...] += lanes(cot)
        xp[:, cols] = jnp.dot(move[...], xs[:, cols], preferred_element_type=f32).astype(bf16)

    prepare(0)
    ones = jnp.ones((slab_rows, chunk), bf16)
    v1, a1, s1, v2, d2, a2, back, d1 = {}, {}, {}, {}, {}, {}, {}, {}

    def x_of(u):
        q, p = divmod(u, pairs)
        return xp[p * deep : (p + 1) * deep, q * chunk : (q + 1) * chunk]

    def first(u):
        v1[u] = jnp.dot(w1p[...], x_of(u), preferred_element_type=f32)

    def first_gelu(u):
        a, both, tail = gelu_parts(v1.pop(u))
        a1[u] = jnp.concatenate([a, ones], axis=0)
        s1[u] = both + tail.astype(f32)

    def second(u):
        v2[u] = jnp.dot(w2x[:, 0 : pair + slab_rows], a1[u], preferred_element_type=f32)

    def second_gelu(u):
        q, p = divmod(u, pairs)
        a2[u], both, tail = gelu_parts(v2.pop(u))
        cot = jnp.concatenate([
            jnp.broadcast_to(cot_ref[2 * p + k : 2 * p + k + 1, q * chunk : (q + 1) * chunk], (hidden, chunk))
            for k in range(2)], axis=0)
        d2[u] = (cot * (both + tail.astype(f32))).astype(bf16)

    def third(u):
        q, p = divmod(u, pairs)
        back[u] = jnp.dot(w2t[...], d2[u], preferred_element_type=f32)
        part = jnp.dot(rox[p], a2[u], preferred_element_type=f32)
        cols = slice(q * chunk, (q + 1) * chunk)
        if p == 0:
            pred_ref[:, cols] = part + rb_ref[0, 0]
        else:
            pred_ref[:, cols] += part
        if u % joint == joint - 1:
            mine = range(u - joint + 1, u + 1)
            acc2[...] += lax.dot_general(
                jnp.concatenate([d2.pop(k) for k in mine], axis=1), jnp.concatenate([a1.pop(k) for k in mine], axis=1),
                NT, preferred_element_type=f32)

    def third_slope(u):
        d1[u] = (back.pop(u) * s1.pop(u)).astype(bf16)

    def fourth(u):
        if u % joint == joint - 1:
            mine = range(u - joint + 1, u + 1)
            both = [jnp.concatenate([d1.pop(k), a2.pop(k)], axis=0) for k in mine]
            acc1[...] += lax.dot_general(
                jnp.concatenate([x_of(k) for k in mine], axis=1), jnp.concatenate(both, axis=1),
                NT, preferred_element_type=f32)

    for i in range(-3, units + 3):
        if (i + 3) % pairs == 2 and (i + 3) // pairs + 1 < chunks:
            prepare((i + 3) // pairs + 1)
        for stage, lag in ((first, 3), (second_gelu, 0), (second, 1), (first_gelu, 2), (third, -1), (third_slope, -2),
                           (fourth, -3)):
            if 0 <= i + lag < units:
                stage(i + lag)

    @pl.when(step == pl.num_programs(0) - 1)
    def _():
        total2 = acc2[...]
        g2 = total2[0:hidden, 0:hidden] + total2[hidden:pair, hidden:pair]
        ro = jnp.sum((iota((hidden, hidden), 0) == iota((hidden, hidden), 1)).astype(f32) * ro_ref[...].astype(f32),
                     axis=1, keepdims=True)
        g2 = 0.25 * ro * g2
        bias = 0.5 * ro * (total2[0:hidden, pair : pair + 1] + total2[hidden:pair, pair : pair + 1])
        eye = iota((hidden, hidden), 0) == iota((hidden, hidden), 1)
        gb2 = jnp.sum(jnp.where(eye, bias, 0.0), axis=0, keepdims=True)
        flat = acc1[...]
        slot = iota((deep, pair), 0)
        side = iota((deep, pair), 1) // hidden
        keep = ((slot % 2 == side) & (slot < half)) | (slot == half)
        weights = jnp.where(keep, flat[:, 0:pair], 0.0)
        reads = jnp.where((slot % 2 == side) & (slot > half + 1), flat[:, pair : 2 * pair], 0.0)
        fold = (iota((pair, hidden), 0) % hidden == iota((pair, hidden), 1)).astype(f32)
        exact = dict(precision=lax.Precision.HIGHEST, preferred_element_type=f32)
        up = jnp.dot(weights, fold, **exact)
        up_r = jnp.dot(reads, fold, **exact)
        joined = jnp.where(iota((cin, deep), 1) // 2 == iota((cin, deep), 0), 1.0, 0.0)
        g1 = jnp.dot(joined, up, **exact)
        gb1 = up[half : half + 1]
        gr = 0.5 * jnp.sum(up_r, axis=0, keepdims=True)
        gb3 = jnp.broadcast_to(jnp.sum(accc[...], keepdims=True), (1, hidden))
        lines = jnp.concatenate([gb1, gr, gb2, gb3, jnp.zeros((cin - 4, hidden), f32)], axis=0)
        body = hidden // 2
        grads_ref[0:body] = jnp.concatenate([g2[0:body], g2[body:hidden]], axis=1)
        grads_ref[body : body + cin] = jnp.concatenate([g1, lines], axis=1)
        rest = grads_ref.shape[0] - body - cin
        grads_ref[body + cin :] = jnp.zeros((rest, 2 * hidden), f32)


def sum_rows(hidden):
    return (hidden // 2 + 8 + 15) // 16 * 16


def mlp(demand, base, feats, cot, w1, b1, w2, b2, ro, rb, width=2048, chunk=256):
    slab_rows, w = demand.shape
    hidden, cin = w1.shape
    packed = (sum_rows(hidden), 2 * hidden)
    pair = 2 * hidden
    depth = cin * slab_rows
    whole = lambda s: pl.BlockSpec(s, lambda i: tuple(0 for _ in s))
    cols = pl.BlockSpec((slab_rows, width), lambda i: (0, i))
    return pl.pallas_call(
        functools.partial(mlp_body, chunk),
        grid=(w // width,),
        in_specs=[
            cols, pl.BlockSpec((1, width), lambda i: (0, i)),
            pl.BlockSpec((cin - 1, slab_rows, width), lambda i: (0, 0, i)), cols,
            whole((cin, hidden)), whole((1, hidden)), whole((hidden, hidden)), whole((1, hidden)), whole((1, hidden)),
            pl.BlockSpec(memory_space=pltpu.SMEM),
        ],
        out_specs=[cols, whole(packed)],
        out_shape=[
            jax.ShapeDtypeStruct((slab_rows, w), f32),
            jax.ShapeDtypeStruct(packed, f32),
        ],
        scratch_shapes=[
            pltpu.VMEM((pair, 4 * cin), bf16),
            pltpu.VMEM((pair, pair + 128), bf16),
            pltpu.VMEM((pair, pair), bf16),
            pltpu.VMEM((slab_rows // 2, slab_rows, pair), bf16),
            pltpu.VMEM((2 * cin * slab_rows, depth + 3 * slab_rows), bf16),
            pltpu.VMEM((depth + 3 * slab_rows, width), bf16),
            pltpu.VMEM((2 * cin * slab_rows, width), bf16),
            pltpu.VMEM((4 * cin, 2 * pair), f32),
            pltpu.VMEM((pair, pair + slab_rows), f32),
            pltpu.VMEM((slab_rows, 128), f32),
        ],
        compiler_params=pltpu.CompilerParams(vmem_limit_bytes=vmem_most),
        name="mlp",
    )(demand, base, feats, cot, w1.T, b1[None, :], w2, b2[None, :], ro[None, :], rb[None, :])


def hail(n):
    me, group = lax.axis_index("canvas"), lax.axis_index("groups")
    barrier = pltpu.get_barrier_semaphore()

    def signal(k, carry):
        pl.semaphore_signal(
            barrier, inc=1, device_id=(group, lax.rem(me + k, n)), device_id_type=pl.DeviceIdType.MESH)
        return carry

    lax.fori_loop(1, n, signal, 0)


def all_here(n):
    pl.semaphore_wait(pltpu.get_barrier_semaphore(), n - 1)


def greet(n):
    hail(n)
    all_here(n)


def swap(n, source, target, send_sem, recv_sem):
    me, group = lax.axis_index("canvas"), lax.axis_index("groups")

    def copy(k, slot):
        peer = lax.rem(me + k, n)
        return pltpu.make_async_remote_copy(
            src_ref=source.at[peer], dst_ref=target.at[slot], send_sem=send_sem.at[k], recv_sem=recv_sem.at[k],
            device_id=(group, peer), device_id_type=pl.DeviceIdType.MESH)

    def start(k, carry):
        copy(k, me).start()
        return carry

    def arrive(k, carry):
        copy(k, lax.rem(me + n - k, n)).wait_recv()
        return carry

    lax.fori_loop(1, n, start, 0)
    target[pl.ds(me, 1)] = source[pl.ds(me, 1)]
    lax.fori_loop(1, n, arrive, 0)

    def finish():
        def left(k, carry):
            copy(k, me).wait_send()
            return carry

        lax.fori_loop(1, n, left, 0)

    return finish


def pack_items(n, slab_rows, w, slabs_ref, offsets_ref, left_ref, span_ref, pins_ref, send_ref):
    cap = send_ref.shape[2]
    one, two = slabs_ref[0:1, :], slabs_ref[1:2, :]
    off_one, off_two = offsets_ref[0:1, :], offsets_ref[1:2, :]
    first_is_low = one <= two
    low, high = jnp.minimum(one, two), jnp.maximum(one, two)
    low_row = jnp.where(first_is_low, off_one, off_two)
    high_row = jnp.where(first_is_low, off_two, off_one)
    left = left_ref[...]
    right = jnp.minimum(left + span_ref[...], w)
    wide = (right - left).astype(f32)
    tall = ((high - low) * slab_rows + high_row - low_row).astype(f32)
    weight = jnp.sqrt(pins_ref[...].astype(f32)) * (wide + tall) / (wide * tall)
    both = lambda x, y: jnp.concatenate([x, y], axis=1)
    slab = both(low, high)
    items = slab.shape[1]
    hot = jnp.where(iota((n, items), 0) == slab, 1.0, 0.0)
    hot_b = hot.astype(bf16)
    span = 256
    upper = (iota((span, span), 0) <= iota((span, span), 1)).astype(bf16)
    blocks = items // span
    before = ((iota((128, items), 1) // span) < iota((128, items), 0)).astype(bf16)
    starts = lax.dot_general(hot_b, before, NT, preferred_element_type=f32)
    counts = []
    for k in range(blocks):
        cols = slice(k * span, (k + 1) * span)
        inside = jnp.dot(hot_b[:, cols], upper, preferred_element_type=f32) + starts[:, k : k + 1]
        counts.append(jnp.sum(inside * hot[:, cols], axis=0, keepdims=True))
    rank = (jnp.concatenate(counts, axis=1) - 1.0).astype(i32)
    spot = jnp.where(iota((cap, items), 0) == rank, 1.0, 0.0).astype(bf16)
    amount = both(weight, -weight)
    coarse = amount.astype(bf16).astype(f32)
    row = both(low_row, high_row).astype(f32)
    start = both(left, left)
    end = both(right, right)
    start_low, end_low = start & 255, end & 255
    kind = iota((4 * n, items), 0) % 4
    mine = (iota((4 * n, items), 0) // 4) == slab

    def field(x0, x1, x2, x3):
        picked = jnp.where(kind == 0, x0, jnp.where(kind == 1, x1, jnp.where(kind == 2, x2, x3)))
        return jnp.where(mine, picked, 0.0).astype(bf16)

    big = field(coarse, row, (start - start_low).astype(f32), (end - end_low).astype(f32))
    small = field(amount - coarse, jnp.zeros_like(row), start_low.astype(f32), end_low.astype(f32))
    table = (lax.dot_general(big, spot, NT, preferred_element_type=f32)
             + lax.dot_general(small, spot, NT, preferred_element_type=f32))
    for d in range(n):
        send_ref[d] = table[4 * d : 4 * d + 4]


def slab(got_ref, local_ref, totals_ref, acc):
    n, _, cap = got_ref.shape
    slab_rows, w = local_ref.shape
    window = 256
    stride = window - 16
    tall = acc.shape[0]
    per = max(1, min(n, 2048 // cap))
    for c in range(n // per):
        def line(which):
            return jnp.concatenate([got_ref[c * per + j, which : which + 1, :] for j in range(per)], axis=1)

        value = line(0).astype(bf16).astype(f32)
        start = line(2)
        group = jnp.floor((start + 0.5) * (1.0 / stride))
        shift = group * stride
        first = (start - shift).astype(i32)
        last = (line(3) - shift).astype(i32)
        key = (group * slab_rows + line(1)).astype(i32)
        count = per * cap
        hot = jnp.where(iota((tall, count), 0) == key, 1.0, 0.0).astype(bf16)
        lane = iota((window, count), 0)
        fine = jnp.where((lane >= first) & (lane < last), value, 0.0).astype(bf16)
        update = lax.dot_general(hot, fine, NT, preferred_element_type=f32)
        if c == 0:
            acc[...] = update
        else:
            acc[...] += update
    tiles = [None] * (w // 128 + 4)
    for g in range(tall // slab_rows):
        at, turn = divmod(g * stride, 128)
        part = jnp.concatenate(
            [acc[g * slab_rows : (g + 1) * slab_rows, :], jnp.zeros((slab_rows, 128), f32)], axis=1)
        if turn:
            part = pltpu.roll(part, turn, 1)
        for k in range(3):
            piece = part[:, k * 128 : (k + 1) * 128]
            tiles[at + k] = piece if tiles[at + k] is None else tiles[at + k] + piece
    rows = iota((slab_rows, 128), 0)
    part = w // n
    for j in range(w // 128):
        t = tiles[j]
        step = 1
        while step < slab_rows:
            t = t + jnp.where(rows >= step, pltpu.roll(t, step, 0), 0.0)
            step *= 2
        local_ref[:, j * 128 : (j + 1) * 128] = t
    for d in range(n):
        totals_ref[d] = local_ref[slab_rows - 1 : slab_rows, d * part : (d + 1) * part]


def route_body(n, slabs_ref, offsets_ref, left_ref, span_ref, pins_ref, local_ref, base_ref,
               send, items, acc, totals, got, result, back, send_a, recv_a, send_b, recv_b, send_c, recv_c):
    hail(n)
    slab_rows, w = local_ref.shape
    pack_items(n, slab_rows, w, slabs_ref, offsets_ref, left_ref, span_ref, pins_ref, send)
    all_here(n)
    end_a = swap(n, send, items, send_a, recv_a)
    slab(items, local_ref, totals, acc)
    end_b = swap(n, totals, got, send_b, recv_b)
    running = jnp.zeros(got.shape[1:], f32)
    for d in range(n):
        result[d] = running
        running = running + got[d]
    end_c = swap(n, result, back, send_c, recv_c)
    part = got.shape[2]
    for d in range(n):
        base_ref[:, d * part : (d + 1) * part] = back[d]
    end_a()
    end_b()
    end_c()


def route(n, slabs, offsets, left, span, pins, slab_rows, w):
    cap = 4 * pins.shape[1] // n
    vmem = pl.BlockSpec(memory_space=pltpu.VMEM)
    part = pltpu.VMEM((n, 1, w // n), f32)
    groups = -(-w // 240)
    return pl.pallas_call(
        functools.partial(route_body, n),
        out_shape=[jax.ShapeDtypeStruct((slab_rows, w), f32), jax.ShapeDtypeStruct((1, w), f32)],
        in_specs=[vmem] * 5,
        out_specs=[vmem] * 2,
        scratch_shapes=[
            pltpu.VMEM((n, 4, cap), f32), pltpu.VMEM((n, 4, cap), f32), pltpu.VMEM((groups * slab_rows, 256), f32),
            part, part, part, part,
        ] + [pltpu.SemaphoreType.DMA((n,))] * 6,
        compiler_params=pltpu.CompilerParams(
            collective_id=0, has_side_effects=True, vmem_limit_bytes=vmem_most),
        name="route",
    )(slabs, offsets, left, span, pins)


def sum_body(n, grads_ref, total_ref, sibling, mine, halves, full, send_sem, recv_sem, pair_send, pair_recv):
    me, group = lax.axis_index("canvas"), lax.axis_index("groups")
    core = lax.rem(me, 2)
    chip = me // 2
    other = me + 1 - 2 * core
    chips = n // 2
    rows = halves.shape[1]
    barrier = pltpu.get_barrier_semaphore()

    def friend(k):
        return 2 * lax.rem(chip + k, chips) + core

    def signal(k, carry):
        pl.semaphore_signal(barrier, inc=1, device_id=(group, friend(k)), device_id_type=pl.DeviceIdType.MESH)
        return carry

    pl.semaphore_signal(barrier, inc=1, device_id=(group, other), device_id_type=pl.DeviceIdType.MESH)
    lax.fori_loop(1, chips, signal, 0)
    pl.semaphore_wait(barrier, chips)

    def hand(source, target, which):
        return pltpu.make_async_remote_copy(
            src_ref=source, dst_ref=target, send_sem=pair_send.at[which], recv_sem=pair_recv.at[which],
            device_id=(group, other), device_id_type=pl.DeviceIdType.MESH)

    first = hand(grads_ref, sibling, 0)
    first.start()
    first.wait_recv()
    mine[...] = grads_ref[...] + sibling[...]
    part = pl.ds(pl.multiple_of(core * rows, 8), rows)

    def copy(k, slot):
        return pltpu.make_async_remote_copy(
            src_ref=mine.at[part], dst_ref=halves.at[slot], send_sem=send_sem.at[k], recv_sem=recv_sem.at[k],
            device_id=(group, friend(k)), device_id_type=pl.DeviceIdType.MESH)

    def start(k, carry):
        copy(k, chip).start()
        return carry

    def arrive(k, carry):
        copy(k, lax.rem(chip + chips - k, chips)).wait_recv()
        return carry

    lax.fori_loop(1, chips, start, 0)
    halves[pl.ds(chip, 1)] = mine[part][None]
    lax.fori_loop(1, chips, arrive, 0)
    total = halves[0]
    for d in range(1, chips):
        total = total + halves[d]
    full[part] = total
    last = hand(full.at[part], full.at[part], 1)
    last.start()

    def left(k, carry):
        copy(k, chip).wait_send()
        return carry

    lax.fori_loop(1, chips, left, 0)
    first.wait_send()
    last.wait()
    total_ref[...] = full[...]


def split_body(cin, total_ref, g1_out, gb1_out, g2_out, gb2_out, gr_out, gb_out,
               g1_ref, gb1_ref, g2_ref, gb2_ref, gr_ref, gb_ref, out_sem):
    hidden = g1_ref.shape[1]
    body = hidden // 2
    g2_ref[0:body] = total_ref[0:body, 0:hidden]
    g2_ref[body:hidden] = total_ref[0:body, hidden:]
    g1_ref[...] = total_ref[body : body + cin, 0:hidden]
    for k, target in enumerate((gb1_ref, gr_ref, gb2_ref)):
        target[...] = total_ref[body + k : body + k + 1, hidden:].reshape(hidden)
    gb_ref[...] = total_ref[body + 3 : body + 4, hidden : hidden + 1].reshape(1)
    pairs = ((g1_ref, g1_out), (gb1_ref, gb1_out), (g2_ref, g2_out), (gb2_ref, gb2_out), (gr_ref, gr_out),
             (gb_ref, gb_out))
    copies = [pltpu.make_async_copy(source, target, out_sem.at[i]) for i, (source, target) in enumerate(pairs)]
    for c in copies:
        c.start()
    for c in copies:
        c.wait()


def sum_all(grads, n, shape):
    hidden, cin = shape
    vmem = pl.BlockSpec(memory_space=pltpu.VMEM)
    line = (hidden,)
    shapes = ((cin, hidden), line, (hidden, hidden), line, line, (1,))
    whole = pltpu.VMEM(grads.shape, f32)
    total = pl.pallas_call(
        functools.partial(sum_body, n),
        out_shape=jax.ShapeDtypeStruct(grads.shape, f32),
        in_specs=[vmem],
        out_specs=vmem,
        scratch_shapes=[whole, whole, pltpu.VMEM((n // 2, grads.shape[0] // 2, grads.shape[1]), f32), whole]
        + [pltpu.SemaphoreType.DMA((n // 2,))] * 2 + [pltpu.SemaphoreType.DMA((2,))] * 2,
        compiler_params=pltpu.CompilerParams(collective_id=1, has_side_effects=True),
        name="sum_all",
    )(grads)
    return pl.pallas_call(
        functools.partial(split_body, cin),
        out_shape=[jax.ShapeDtypeStruct(shape, f32) for shape in shapes],
        in_specs=[vmem],
        out_specs=[pl.BlockSpec(memory_space=pltpu.HBM)] * 6,
        scratch_shapes=[pltpu.VMEM(shape, f32) for shape in shapes] + [pltpu.SemaphoreType.DMA((6,))],
        name="split",
    )(total)


def per_device(
    net_slabs,
    row_offsets,
    left_column,
    column_span,
    pin_counts,
    tile_features,
    cotangent,
    first_weight,
    first_bias,
    second_weight,
    second_bias,
    readout_weight,
    readout_bias,
):
    devices = lax.axis_size("canvas")
    slab_rows = tile_features.shape[1]
    canvas_width = tile_features.shape[2]
    local, base = route(
        devices, net_slabs.T, row_offsets.T, left_column[None, :], column_span[None, :], pin_counts[None, :],
        slab_rows, canvas_width)
    prediction, grads = mlp(
        local, base, tile_features, cotangent, first_weight, first_bias, second_weight, second_bias,
        readout_weight, readout_bias)
    g1, gb1, g2, gb2, gr, gb = sum_all(grads, devices, first_weight.shape)
    return (prediction, g1.T, gb1, g2, gb2, gr, gb)


def solution(mesh):
    in_specs = (
        P(("groups", "canvas"), None),
        P(("groups", "canvas"), None),
        P(("groups", "canvas")),
        P(("groups", "canvas")),
        P(("groups", "canvas")),
        P(None, ("groups", "canvas"), None),
        P(("groups", "canvas"), None),
        P(),
        P(),
        P(),
        P(),
        P(),
        P(),
    )
    out_specs = (
        P(("groups", "canvas"), None),
        P("groups", None),
        P("groups"),
        P("groups", None),
        P("groups"),
        P("groups"),
        P("groups"),
    )
    return jax.shard_map(
        per_device, mesh=mesh, in_specs=in_specs, out_specs=out_specs, check_vma=False
    )
```

```python
import functools
import jax
import jax.numpy as jnp
from jax import lax
from jax.experimental import pallas as pl
from jax.experimental.pallas import tpu as pltpu
from jax.sharding import PartitionSpec as P

root_half = 0.7071067811865476
log2_two_over_root_pi = 0.17425071
log2e = 1.4426950408889634
vmem_most = 60 * 1024 * 1024
f32 = jnp.float32
bf16 = jnp.bfloat16
i32 = jnp.int32
NT = (((1,), (1,)), ((), ()))


def iota(shape, dim):
    return lax.broadcasted_iota(i32, shape, dim)


def lanes(a):
    return sum(a[:, k * 128 : (k + 1) * 128] for k in range(a.shape[1] // 128))


def gelu_parts(v):
    w = v * root_half
    both = 1.0 + lax.erf(w)
    w = w.astype(bf16)
    tail = w * jnp.exp2((w * w) * bf16(-log2e) + bf16(log2_two_over_root_pi))
    return (v * both).astype(bf16), both, tail


def split_column(b):
    high = b.astype(bf16).astype(f32)
    return high, b - high


def mlp_body(chunk, demand_ref, base_ref, feat_ref, cot_ref, w1_ref, b1_ref, w2_ref, b2_ref, ro_ref, rb_ref,
             pred_ref, grads_ref,
             w1p, w2x, w2t, rox, move, xs, xp, acc1, acc2, accc):
    step = pl.program_id(0)
    slab_rows, width = demand_ref.shape
    cin, hidden = w1_ref.shape
    pair = 2 * hidden
    pairs = slab_rows // 2
    depth = cin * slab_rows
    deep = 4 * cin
    half = 2 * cin
    reach = xs.shape[0]

    @pl.when(step == 0)
    def _():
        pick = (iota((pair, hidden), 0) % hidden == iota((pair, hidden), 1)).astype(bf16)
        pick_f = pick.astype(f32)
        spread = (iota((cin, deep), 1) // 2 == iota((cin, deep), 0)).astype(bf16)
        tall = lax.dot_general(pick, w1_ref[...], NT, preferred_element_type=f32).astype(bf16)
        wide = jnp.dot(tall, spread, preferred_element_type=f32)
        high, low = split_column(jnp.sum(pick_f * b1_ref[...], axis=1, keepdims=True))
        lane = iota((pair, deep), 1)
        keep = iota((pair, deep), 0) // hidden == lane % 2
        w1p[...] = jnp.where(
            lane == half, high, jnp.where(lane == half + 1, low, jnp.where(keep, wide, 0.0))).astype(bf16)
        same = iota((pair, pair), 0) // hidden == iota((pair, pair), 1) // hidden
        down = jnp.dot(pick, w2_ref[...], preferred_element_type=f32).astype(bf16)
        full = lax.dot_general(down, pick, NT, preferred_element_type=f32)
        w2x[:, 0:pair] = jnp.where(same, 0.5 * full, 0.0).astype(bf16)
        high, low = split_column(jnp.sum(pick_f * b2_ref[...], axis=1, keepdims=True))
        lane = iota((pair, 128), 1)
        w2x[:, pair : pair + 128] = jnp.where(lane == 0, high, jnp.where(lane == 1, low, 0.0)).astype(bf16)
        flip = lax.dot_general(pick, w2_ref[...], NT, preferred_element_type=f32).astype(bf16)
        full_t = lax.dot_general(flip, pick, NT, preferred_element_type=f32)
        ro_wide = lax.dot_general(ro_ref[...], pick, NT, preferred_element_type=f32)
        w2t[...] = jnp.where(same, 0.25 * full_t * ro_wide, 0.0).astype(bf16)
        ro_rows = 0.5 * jnp.broadcast_to(ro_wide, (slab_rows, pair))
        for p in range(pairs):
            here = iota((slab_rows, pair), 0) == iota((slab_rows, pair), 1) // hidden + 2 * p
            rox[p] = jnp.where(here, ro_rows, 0.0).astype(bf16)
        line = iota((pairs * deep, reach), 0)
        slot = line % deep
        row = 2 * (line // deep) + slot % 2
        source = jnp.where(slot < half, (slot // 2) * slab_rows + row,
                           jnp.where(slot < half + 2, depth + 2 * slab_rows,
                                     jnp.where(slot < half + 6, depth + (slot // 2 - cin - 1) * slab_rows + row, -1)))
        move[...] = (iota((pairs * deep, reach), 1) == source).astype(bf16)
        acc1[...] = jnp.zeros_like(acc1)
        acc2[...] = jnp.zeros_like(acc2)
        accc[...] = jnp.zeros_like(accc)
        xs[depth + 2 * slab_rows : reach, :] = jnp.ones((reach - depth - 2 * slab_rows, width), bf16)

    chunks = width // chunk
    units = pairs * chunks
    joint = 4

    def prepare(q):
        cols = slice(q * chunk, (q + 1) * chunk)
        cot = cot_ref[:, cols]
        high = cot.astype(bf16)
        xs[0:slab_rows, cols] = jnp.log(1.0 + (demand_ref[:, cols] + base_ref[:, cols])).astype(bf16)
        xs[slab_rows:depth, cols] = feat_ref[:, :, cols].reshape((cin - 1) * slab_rows, chunk)
        xs[depth : depth + slab_rows, cols] = high
        xs[depth + slab_rows : depth + 2 * slab_rows, cols] = (cot - high.astype(f32)).astype(bf16)
        accc[...] += lanes(cot)
        xp[:, cols] = jnp.dot(move[...], xs[:, cols], preferred_element_type=f32).astype(bf16)

    prepare(0)
    ones = jnp.ones((slab_rows, chunk), bf16)
    v1, a1, s1, v2, d2, a2, back, d1 = {}, {}, {}, {}, {}, {}, {}, {}

    def x_of(u):
        q, p = divmod(u, pairs)
        return xp[p * deep : (p + 1) * deep, q * chunk : (q + 1) * chunk]

    def first(u):
        v1[u] = jnp.dot(w1p[...], x_of(u), preferred_element_type=f32)

    def first_gelu(u):
        a, both, tail = gelu_parts(v1.pop(u))
        a1[u] = jnp.concatenate([a, ones], axis=0)
        s1[u] = both + tail.astype(f32)

    def second(u):
        v2[u] = jnp.dot(w2x[:, 0 : pair + slab_rows], a1[u], preferred_element_type=f32)

    def second_gelu(u):
        q, p = divmod(u, pairs)
        a2[u], both, tail = gelu_parts(v2.pop(u))
        cot = jnp.concatenate([
            jnp.broadcast_to(cot_ref[2 * p + k : 2 * p + k + 1, q * chunk : (q + 1) * chunk], (hidden, chunk))
            for k in range(2)], axis=0)
        d2[u] = (cot * (both + tail.astype(f32))).astype(bf16)

    def third(u):
        q, p = divmod(u, pairs)
        back[u] = jnp.dot(w2t[...], d2[u], preferred_element_type=f32)
        part = jnp.dot(rox[p], a2[u], preferred_element_type=f32)
        cols = slice(q * chunk, (q + 1) * chunk)
        if p == 0:
            pred_ref[:, cols] = part + rb_ref[0, 0]
        else:
            pred_ref[:, cols] += part
        if u % joint == joint - 1:
            mine = range(u - joint + 1, u + 1)
            acc2[...] += lax.dot_general(
                jnp.concatenate([d2.pop(k) for k in mine], axis=1), jnp.concatenate([a1.pop(k) for k in mine], axis=1),
                NT, preferred_element_type=f32)

    def third_slope(u):
        d1[u] = (back.pop(u) * s1.pop(u)).astype(bf16)

    def fourth(u):
        if u % joint == joint - 1:
            mine = range(u - joint + 1, u + 1)
            both = [jnp.concatenate([d1.pop(k), a2.pop(k)], axis=0) for k in mine]
            acc1[...] += lax.dot_general(
                jnp.concatenate([x_of(k) for k in mine], axis=1), jnp.concatenate(both, axis=1),
                NT, preferred_element_type=f32)

    for i in range(-3, units + 3):
        if (i + 3) % pairs == 2 and (i + 3) // pairs + 1 < chunks:
            prepare((i + 3) // pairs + 1)
        for stage, lag in ((first, 3), (second_gelu, 0), (second, 1), (first_gelu, 2), (third, -1), (third_slope, -2),
                           (fourth, -3)):
            if 0 <= i + lag < units:
                stage(i + lag)

    @pl.when(step == pl.num_programs(0) - 1)
    def _():
        total2 = acc2[...]
        g2 = total2[0:hidden, 0:hidden] + total2[hidden:pair, hidden:pair]
        ro = jnp.sum((iota((hidden, hidden), 0) == iota((hidden, hidden), 1)).astype(f32) * ro_ref[...].astype(f32),
                     axis=1, keepdims=True)
        g2 = 0.25 * ro * g2
        bias = 0.5 * ro * (total2[0:hidden, pair : pair + 1] + total2[hidden:pair, pair : pair + 1])
        eye = iota((hidden, hidden), 0) == iota((hidden, hidden), 1)
        gb2 = jnp.sum(jnp.where(eye, bias, 0.0), axis=0, keepdims=True)
        flat = acc1[...]
        slot = iota((deep, pair), 0)
        side = iota((deep, pair), 1) // hidden
        keep = ((slot % 2 == side) & (slot < half)) | (slot == half)
        weights = jnp.where(keep, flat[:, 0:pair], 0.0)
        reads = jnp.where((slot % 2 == side) & (slot > half + 1), flat[:, pair : 2 * pair], 0.0)
        fold = (iota((pair, hidden), 0) % hidden == iota((pair, hidden), 1)).astype(f32)
        exact = dict(precision=lax.Precision.HIGHEST, preferred_element_type=f32)
        up = jnp.dot(weights, fold, **exact)
        up_r = jnp.dot(reads, fold, **exact)
        joined = jnp.where(iota((cin, deep), 1) // 2 == iota((cin, deep), 0), 1.0, 0.0)
        g1 = jnp.dot(joined, up, **exact)
        gb1 = up[half : half + 1]
        gr = 0.5 * jnp.sum(up_r, axis=0, keepdims=True)
        gb3 = jnp.broadcast_to(jnp.sum(accc[...], keepdims=True), (1, hidden))
        lines = jnp.concatenate([gb1, gr, gb2, gb3, jnp.zeros((cin - 4, hidden), f32)], axis=0)
        body = hidden // 2
        grads_ref[0:body] = jnp.concatenate([g2[0:body], g2[body:hidden]], axis=1)
        grads_ref[body : body + cin] = jnp.concatenate([g1, lines], axis=1)
        rest = grads_ref.shape[0] - body - cin
        grads_ref[body + cin :] = jnp.zeros((rest, 2 * hidden), f32)


def sum_rows(hidden):
    return (hidden // 2 + 8 + 15) // 16 * 16


def mlp(demand, base, feats, cot, w1, b1, w2, b2, ro, rb, width=2048, chunk=256):
    slab_rows, w = demand.shape
    hidden, cin = w1.shape
    packed = (sum_rows(hidden), 2 * hidden)
    pair = 2 * hidden
    depth = cin * slab_rows
    whole = lambda s: pl.BlockSpec(s, lambda i: tuple(0 for _ in s))
    cols = pl.BlockSpec((slab_rows, width), lambda i: (0, i))
    return pl.pallas_call(
        functools.partial(mlp_body, chunk),
        grid=(w // width,),
        in_specs=[
            cols, pl.BlockSpec((1, width), lambda i: (0, i)),
            pl.BlockSpec((cin - 1, slab_rows, width), lambda i: (0, 0, i)), cols,
            whole((cin, hidden)), whole((1, hidden)), whole((hidden, hidden)), whole((1, hidden)), whole((1, hidden)),
            pl.BlockSpec(memory_space=pltpu.SMEM),
        ],
        out_specs=[cols, whole(packed)],
        out_shape=[
            jax.ShapeDtypeStruct((slab_rows, w), f32),
            jax.ShapeDtypeStruct(packed, f32),
        ],
        scratch_shapes=[
            pltpu.VMEM((pair, 4 * cin), bf16),
            pltpu.VMEM((pair, pair + 128), bf16),
            pltpu.VMEM((pair, pair), bf16),
            pltpu.VMEM((slab_rows // 2, slab_rows, pair), bf16),
            pltpu.VMEM((2 * cin * slab_rows, depth + 3 * slab_rows), bf16),
            pltpu.VMEM((depth + 3 * slab_rows, width), bf16),
            pltpu.VMEM((2 * cin * slab_rows, width), bf16),
            pltpu.VMEM((4 * cin, 2 * pair), f32),
            pltpu.VMEM((pair, pair + slab_rows), f32),
            pltpu.VMEM((slab_rows, 128), f32),
        ],
        compiler_params=pltpu.CompilerParams(vmem_limit_bytes=vmem_most),
        name="mlp",
    )(demand, base, feats, cot, w1.T, b1[None, :], w2, b2[None, :], ro[None, :], rb[None, :])


def hail(n):
    me, group = lax.axis_index("canvas"), lax.axis_index("groups")
    barrier = pltpu.get_barrier_semaphore()

    def signal(k, carry):
        pl.semaphore_signal(
            barrier, inc=1, device_id=(group, lax.rem(me + k, n)), device_id_type=pl.DeviceIdType.MESH)
        return carry

    lax.fori_loop(1, n, signal, 0)


def all_here(n):
    pl.semaphore_wait(pltpu.get_barrier_semaphore(), n - 1)


def greet(n):
    hail(n)
    all_here(n)


def swap(n, source, target, send_sem, recv_sem):
    me, group = lax.axis_index("canvas"), lax.axis_index("groups")

    def copy(k, slot):
        peer = lax.rem(me + k, n)
        return pltpu.make_async_remote_copy(
            src_ref=source.at[peer], dst_ref=target.at[slot], send_sem=send_sem.at[k], recv_sem=recv_sem.at[k],
            device_id=(group, peer), device_id_type=pl.DeviceIdType.MESH)

    def start(k, carry):
        copy(k, me).start()
        return carry

    def arrive(k, carry):
        copy(k, lax.rem(me + n - k, n)).wait_recv()
        return carry

    lax.fori_loop(1, n, start, 0)
    target[pl.ds(me, 1)] = source[pl.ds(me, 1)]
    lax.fori_loop(1, n, arrive, 0)

    def finish():
        def left(k, carry):
            copy(k, me).wait_send()
            return carry

        lax.fori_loop(1, n, left, 0)

    return finish


def pack_items(n, slab_rows, w, slabs_ref, offsets_ref, left_ref, span_ref, pins_ref, send_ref):
    cap = send_ref.shape[2]
    one, two = slabs_ref[0:1, :], slabs_ref[1:2, :]
    off_one, off_two = offsets_ref[0:1, :], offsets_ref[1:2, :]
    first_is_low = one <= two
    low, high = jnp.minimum(one, two), jnp.maximum(one, two)
    low_row = jnp.where(first_is_low, off_one, off_two)
    high_row = jnp.where(first_is_low, off_two, off_one)
    left = left_ref[...]
    right = jnp.minimum(left + span_ref[...], w)
    wide = (right - left).astype(f32)
    tall = ((high - low) * slab_rows + high_row - low_row).astype(f32)
    weight = jnp.sqrt(pins_ref[...].astype(f32)) * (wide + tall) / (wide * tall)
    both = lambda x, y: jnp.concatenate([x, y], axis=1)
    slab = both(low, high)
    items = slab.shape[1]
    hot = jnp.where(iota((n, items), 0) == slab, 1.0, 0.0)
    hot_b = hot.astype(bf16)
    span = 256
    upper = (iota((span, span), 0) <= iota((span, span), 1)).astype(bf16)
    blocks = items // span
    before = ((iota((128, items), 1) // span) < iota((128, items), 0)).astype(bf16)
    starts = lax.dot_general(hot_b, before, NT, preferred_element_type=f32)
    counts = []
    for k in range(blocks):
        cols = slice(k * span, (k + 1) * span)
        inside = jnp.dot(hot_b[:, cols], upper, preferred_element_type=f32) + starts[:, k : k + 1]
        counts.append(jnp.sum(inside * hot[:, cols], axis=0, keepdims=True))
    rank = (jnp.concatenate(counts, axis=1) - 1.0).astype(i32)
    spot = jnp.where(iota((cap, items), 0) == rank, 1.0, 0.0).astype(bf16)
    amount = both(weight, -weight)
    coarse = amount.astype(bf16).astype(f32)
    row = both(low_row, high_row).astype(f32)
    start = both(left, left)
    end = both(right, right)
    start_low, end_low = start & 255, end & 255
    kind = iota((4 * n, items), 0) % 4
    mine = (iota((4 * n, items), 0) // 4) == slab

    def field(x0, x1, x2, x3):
        picked = jnp.where(kind == 0, x0, jnp.where(kind == 1, x1, jnp.where(kind == 2, x2, x3)))
        return jnp.where(mine, picked, 0.0).astype(bf16)

    big = field(coarse, row, (start - start_low).astype(f32), (end - end_low).astype(f32))
    small = field(amount - coarse, jnp.zeros_like(row), start_low.astype(f32), end_low.astype(f32))
    table = (lax.dot_general(big, spot, NT, preferred_element_type=f32)
             + lax.dot_general(small, spot, NT, preferred_element_type=f32))
    for d in range(n):
        send_ref[d] = table[4 * d : 4 * d + 4]


def slab(got_ref, local_ref, totals_ref, acc):
    n, _, cap = got_ref.shape
    slab_rows, w = local_ref.shape
    window = 256
    stride = window - 16
    tall = acc.shape[0]
    per = max(1, min(n, 2048 // cap))
    for c in range(n // per):
        def line(which):
            return jnp.concatenate([got_ref[c * per + j, which : which + 1, :] for j in range(per)], axis=1)

        value = line(0).astype(bf16)
        start = line(2)
        group = jnp.floor((start + 0.5) * (1.0 / stride))
        shift = group * stride
        first = (start - shift).astype(bf16)
        last = (line(3) - shift).astype(bf16)
        count = per * cap
        group = jnp.broadcast_to(group, (slab_rows, count)).astype(bf16)
        own_row = jnp.where(iota((slab_rows, count), 0).astype(f32) == line(1), 1.0, 0.0).astype(bf16)
        zero = jnp.zeros((slab_rows, count), bf16)
        hot = jnp.concatenate(
            [jnp.where(group == bf16(g), own_row, zero) for g in range(tall // slab_rows)], axis=0)
        lane = iota((window, count), 0).astype(f32).astype(bf16)
        fine = jnp.where((lane >= first) & (lane < last), value, jnp.zeros((window, count), bf16))
        update = lax.dot_general(hot, fine, NT, preferred_element_type=f32)
        if c == 0:
            acc[...] = update
        else:
            acc[...] += update
    tiles = [None] * (w // 128 + 4)
    for g in range(tall // slab_rows):
        at, turn = divmod(g * stride, 128)
        part = jnp.concatenate(
            [acc[g * slab_rows : (g + 1) * slab_rows, :], jnp.zeros((slab_rows, 128), f32)], axis=1)
        if turn:
            part = pltpu.roll(part, turn, 1)
        for k in range(3):
            piece = part[:, k * 128 : (k + 1) * 128]
            tiles[at + k] = piece if tiles[at + k] is None else tiles[at + k] + piece
    rows = iota((slab_rows, 128), 0)
    part = w // n
    for j in range(w // 128):
        t = tiles[j]
        step = 1
        while step < slab_rows:
            t = t + jnp.where(rows >= step, pltpu.roll(t, step, 0), 0.0)
            step *= 2
        local_ref[:, j * 128 : (j + 1) * 128] = t
    for d in range(n):
        totals_ref[d] = local_ref[slab_rows - 1 : slab_rows, d * part : (d + 1) * part]


def route_body(n, slabs_ref, offsets_ref, left_ref, span_ref, pins_ref, local_ref, base_ref,
               send, items, acc, totals, got, result, back, send_a, recv_a, send_b, recv_b, send_c, recv_c):
    hail(n)
    slab_rows, w = local_ref.shape
    pack_items(n, slab_rows, w, slabs_ref, offsets_ref, left_ref, span_ref, pins_ref, send)
    all_here(n)
    end_a = swap(n, send, items, send_a, recv_a)
    slab(items, local_ref, totals, acc)
    end_b = swap(n, totals, got, send_b, recv_b)
    running = jnp.zeros(got.shape[1:], f32)
    for d in range(n):
        result[d] = running
        running = running + got[d]
    end_c = swap(n, result, back, send_c, recv_c)
    part = got.shape[2]
    for d in range(n):
        base_ref[:, d * part : (d + 1) * part] = back[d]
    end_a()
    end_b()
    end_c()


def route(n, slabs, offsets, left, span, pins, slab_rows, w):
    cap = 4 * pins.shape[1] // n
    vmem = pl.BlockSpec(memory_space=pltpu.VMEM)
    part = pltpu.VMEM((n, 1, w // n), f32)
    groups = -(-w // 240)
    return pl.pallas_call(
        functools.partial(route_body, n),
        out_shape=[jax.ShapeDtypeStruct((slab_rows, w), f32), jax.ShapeDtypeStruct((1, w), f32)],
        in_specs=[vmem] * 5,
        out_specs=[vmem] * 2,
        scratch_shapes=[
            pltpu.VMEM((n, 4, cap), f32), pltpu.VMEM((n, 4, cap), f32), pltpu.VMEM((groups * slab_rows, 256), f32),
            part, part, part, part,
        ] + [pltpu.SemaphoreType.DMA((n,))] * 6,
        compiler_params=pltpu.CompilerParams(
            collective_id=0, has_side_effects=True, vmem_limit_bytes=vmem_most),
        name="route",
    )(slabs, offsets, left, span, pins)


def sum_body(n, grads_ref, total_ref, sibling, mine, halves, full, send_sem, recv_sem, pair_send, pair_recv):
    me, group = lax.axis_index("canvas"), lax.axis_index("groups")
    core = lax.rem(me, 2)
    chip = me // 2
    other = me + 1 - 2 * core
    chips = n // 2
    rows = halves.shape[1]
    barrier = pltpu.get_barrier_semaphore()

    def friend(k):
        return 2 * lax.rem(chip + k, chips) + core

    def signal(k, carry):
        pl.semaphore_signal(barrier, inc=1, device_id=(group, friend(k)), device_id_type=pl.DeviceIdType.MESH)
        return carry

    pl.semaphore_signal(barrier, inc=1, device_id=(group, other), device_id_type=pl.DeviceIdType.MESH)
    lax.fori_loop(1, chips, signal, 0)
    pl.semaphore_wait(barrier, chips)

    def hand(source, target, which):
        return pltpu.make_async_remote_copy(
            src_ref=source, dst_ref=target, send_sem=pair_send.at[which], recv_sem=pair_recv.at[which],
            device_id=(group, other), device_id_type=pl.DeviceIdType.MESH)

    first = hand(grads_ref, sibling, 0)
    first.start()
    first.wait_recv()
    mine[...] = grads_ref[...] + sibling[...]
    part = pl.ds(pl.multiple_of(core * rows, 8), rows)

    def copy(k, slot):
        return pltpu.make_async_remote_copy(
            src_ref=mine.at[part], dst_ref=halves.at[slot], send_sem=send_sem.at[k], recv_sem=recv_sem.at[k],
            device_id=(group, friend(k)), device_id_type=pl.DeviceIdType.MESH)

    def start(k, carry):
        copy(k, chip).start()
        return carry

    def arrive(k, carry):
        copy(k, lax.rem(chip + chips - k, chips)).wait_recv()
        return carry

    lax.fori_loop(1, chips, start, 0)
    halves[pl.ds(chip, 1)] = mine[part][None]
    lax.fori_loop(1, chips, arrive, 0)
    total = halves[0]
    for d in range(1, chips):
        total = total + halves[d]
    full[part] = total
    last = hand(full.at[part], full.at[part], 1)
    last.start()

    def left(k, carry):
        copy(k, chip).wait_send()
        return carry

    lax.fori_loop(1, chips, left, 0)
    first.wait_send()
    last.wait()
    total_ref[...] = full[...]


def split_body(cin, total_ref, g1_out, gb1_out, g2_out, gb2_out, gr_out, gb_out,
               g1_ref, gb1_ref, g2_ref, gb2_ref, gr_ref, gb_ref, out_sem):
    hidden = g1_ref.shape[1]
    body = hidden // 2
    g2_ref[0:body] = total_ref[0:body, 0:hidden]
    g2_ref[body:hidden] = total_ref[0:body, hidden:]
    g1_ref[...] = total_ref[body : body + cin, 0:hidden]
    for k, target in enumerate((gb1_ref, gr_ref, gb2_ref)):
        target[...] = total_ref[body + k : body + k + 1, hidden:].reshape(hidden)
    gb_ref[...] = total_ref[body + 3 : body + 4, hidden : hidden + 1].reshape(1)
    pairs = ((g1_ref, g1_out), (gb1_ref, gb1_out), (g2_ref, g2_out), (gb2_ref, gb2_out), (gr_ref, gr_out),
             (gb_ref, gb_out))
    copies = [pltpu.make_async_copy(source, target, out_sem.at[i]) for i, (source, target) in enumerate(pairs)]
    for c in copies:
        c.start()
    for c in copies:
        c.wait()


def sum_all(grads, n, shape):
    hidden, cin = shape
    vmem = pl.BlockSpec(memory_space=pltpu.VMEM)
    line = (hidden,)
    shapes = ((cin, hidden), line, (hidden, hidden), line, line, (1,))
    whole = pltpu.VMEM(grads.shape, f32)
    total = pl.pallas_call(
        functools.partial(sum_body, n),
        out_shape=jax.ShapeDtypeStruct(grads.shape, f32),
        in_specs=[vmem],
        out_specs=vmem,
        scratch_shapes=[whole, whole, pltpu.VMEM((n // 2, grads.shape[0] // 2, grads.shape[1]), f32), whole]
        + [pltpu.SemaphoreType.DMA((n // 2,))] * 2 + [pltpu.SemaphoreType.DMA((2,))] * 2,
        compiler_params=pltpu.CompilerParams(collective_id=1, has_side_effects=True),
        name="sum_all",
    )(grads)
    return pl.pallas_call(
        functools.partial(split_body, cin),
        out_shape=[jax.ShapeDtypeStruct(shape, f32) for shape in shapes],
        in_specs=[vmem],
        out_specs=[pl.BlockSpec(memory_space=pltpu.HBM)] * 6,
        scratch_shapes=[pltpu.VMEM(shape, f32) for shape in shapes] + [pltpu.SemaphoreType.DMA((6,))],
        name="split",
    )(total)


def per_device(
    net_slabs,
    row_offsets,
    left_column,
    column_span,
    pin_counts,
    tile_features,
    cotangent,
    first_weight,
    first_bias,
    second_weight,
    second_bias,
    readout_weight,
    readout_bias,
):
    devices = lax.axis_size("canvas")
    slab_rows = tile_features.shape[1]
    canvas_width = tile_features.shape[2]
    local, base = route(
        devices, net_slabs.T, row_offsets.T, left_column[None, :], column_span[None, :], pin_counts[None, :],
        slab_rows, canvas_width)
    prediction, grads = mlp(
        local, base, tile_features, cotangent, first_weight, first_bias, second_weight, second_bias,
        readout_weight, readout_bias)
    g1, gb1, g2, gb2, gr, gb = sum_all(grads, devices, first_weight.shape)
    return (prediction, g1.T, gb1, g2, gb2, gr, gb)


def solution(mesh):
    in_specs = (
        P(("groups", "canvas"), None),
        P(("groups", "canvas"), None),
        P(("groups", "canvas")),
        P(("groups", "canvas")),
        P(("groups", "canvas")),
        P(None, ("groups", "canvas"), None),
        P(("groups", "canvas"), None),
        P(),
        P(),
        P(),
        P(),
        P(),
        P(),
    )
    out_specs = (
        P(("groups", "canvas"), None),
        P("groups", None),
        P("groups"),
        P("groups", None),
        P("groups"),
        P("groups"),
        P("groups"),
    )
    return jax.shard_map(
        per_device, mesh=mesh, in_specs=in_specs, out_specs=out_specs, check_vma=False
    )
```

```python
import functools
import jax
import jax.numpy as jnp
from jax import lax
from jax.experimental import pallas as pl
from jax.experimental.pallas import tpu as pltpu
from jax.sharding import PartitionSpec as P

root_half = 0.7071067811865476
log2_two_over_root_pi = 0.17425071
log2e = 1.4426950408889634
vmem_most = 60 * 1024 * 1024
f32 = jnp.float32
bf16 = jnp.bfloat16
i32 = jnp.int32
NT = (((1,), (1,)), ((), ()))


def iota(shape, dim):
    return lax.broadcasted_iota(i32, shape, dim)


def lanes(a):
    return sum(a[:, k * 128 : (k + 1) * 128] for k in range(a.shape[1] // 128))


def gelu_parts(v):
    w = v * root_half
    both = 1.0 + lax.erf(w)
    w = w.astype(bf16)
    tail = w * jnp.exp2((w * w) * bf16(-log2e) + bf16(log2_two_over_root_pi))
    return (v * both).astype(bf16), both, tail


def split_column(b):
    high = b.astype(bf16).astype(f32)
    return high, b - high


def mlp_body(chunk, demand_ref, base_ref, feat_ref, cot_ref, w1_ref, b1_ref, w2_ref, b2_ref, ro_ref, rb_ref,
             pred_ref, grads_ref,
             w1p, w2x, w2t, rox, move, xs, xp, acc1, acc2, accc):
    step = pl.program_id(0)
    slab_rows, width = demand_ref.shape
    cin, hidden = w1_ref.shape
    pair = 2 * hidden
    pairs = slab_rows // 2
    depth = cin * slab_rows
    deep = 4 * cin
    half = 2 * cin
    reach = xs.shape[0]

    @pl.when(step == 0)
    def _():
        pick = (iota((pair, hidden), 0) % hidden == iota((pair, hidden), 1)).astype(bf16)
        pick_f = pick.astype(f32)
        spread = (iota((cin, deep), 1) // 2 == iota((cin, deep), 0)).astype(bf16)
        tall = lax.dot_general(pick, w1_ref[...], NT, preferred_element_type=f32).astype(bf16)
        wide = jnp.dot(tall, spread, preferred_element_type=f32)
        high, low = split_column(jnp.sum(pick_f * b1_ref[...], axis=1, keepdims=True))
        lane = iota((pair, deep), 1)
        keep = iota((pair, deep), 0) // hidden == lane % 2
        w1p[...] = jnp.where(
            lane == half, high, jnp.where(lane == half + 1, low, jnp.where(keep, wide, 0.0))).astype(bf16)
        same = iota((pair, pair), 0) // hidden == iota((pair, pair), 1) // hidden
        down = jnp.dot(pick, w2_ref[...], preferred_element_type=f32).astype(bf16)
        full = lax.dot_general(down, pick, NT, preferred_element_type=f32)
        w2x[:, 0:pair] = jnp.where(same, 0.5 * full, 0.0).astype(bf16)
        high, low = split_column(jnp.sum(pick_f * b2_ref[...], axis=1, keepdims=True))
        lane = iota((pair, 128), 1)
        w2x[:, pair : pair + 128] = jnp.where(lane == 0, high, jnp.where(lane == 1, low, 0.0)).astype(bf16)
        flip = lax.dot_general(pick, w2_ref[...], NT, preferred_element_type=f32).astype(bf16)
        full_t = lax.dot_general(flip, pick, NT, preferred_element_type=f32)
        ro_wide = lax.dot_general(ro_ref[...], pick, NT, preferred_element_type=f32)
        w2t[...] = jnp.where(same, 0.25 * full_t * ro_wide, 0.0).astype(bf16)
        ro_rows = 0.5 * jnp.broadcast_to(ro_wide, (slab_rows, pair))
        for p in range(pairs):
            here = iota((slab_rows, pair), 0) == iota((slab_rows, pair), 1) // hidden + 2 * p
            rox[p] = jnp.where(here, ro_rows, 0.0).astype(bf16)
        line = iota((pairs * deep, reach), 0)
        slot = line % deep
        row = 2 * (line // deep) + slot % 2
        source = jnp.where(slot < half, (slot // 2) * slab_rows + row,
                           jnp.where(slot < half + 2, depth + 2 * slab_rows,
                                     jnp.where(slot < half + 6, depth + (slot // 2 - cin - 1) * slab_rows + row, -1)))
        move[...] = (iota((pairs * deep, reach), 1) == source).astype(bf16)
        acc1[...] = jnp.zeros_like(acc1)
        acc2[...] = jnp.zeros_like(acc2)
        accc[...] = jnp.zeros_like(accc)
        xs[depth + 2 * slab_rows : reach, :] = jnp.ones((reach - depth - 2 * slab_rows, width), bf16)

    chunks = width // chunk
    units = pairs * chunks
    joint = 4

    def prepare(q):
        cols = slice(q * chunk, (q + 1) * chunk)
        cot = cot_ref[:, cols]
        high = cot.astype(bf16)
        xs[0:slab_rows, cols] = jnp.log(1.0 + (demand_ref[:, cols] + base_ref[:, cols])).astype(bf16)
        xs[slab_rows:depth, cols] = feat_ref[:, :, cols].reshape((cin - 1) * slab_rows, chunk)
        xs[depth : depth + slab_rows, cols] = high
        xs[depth + slab_rows : depth + 2 * slab_rows, cols] = (cot - high.astype(f32)).astype(bf16)
        accc[...] += lanes(cot)
        xp[:, cols] = jnp.dot(move[...], xs[:, cols], preferred_element_type=f32).astype(bf16)

    prepare(0)
    ones = jnp.ones((slab_rows, chunk), bf16)
    v1, a1, s1, v2, d2, a2, back, d1 = {}, {}, {}, {}, {}, {}, {}, {}

    def x_of(u):
        q, p = divmod(u, pairs)
        return xp[p * deep : (p + 1) * deep, q * chunk : (q + 1) * chunk]

    def first(u):
        v1[u] = jnp.dot(w1p[...], x_of(u), preferred_element_type=f32)

    def first_gelu(u):
        a, both, tail = gelu_parts(v1.pop(u))
        a1[u] = jnp.concatenate([a, ones], axis=0)
        s1[u] = both + tail.astype(f32)

    def second(u):
        v2[u] = jnp.dot(w2x[:, 0 : pair + slab_rows], a1[u], preferred_element_type=f32)

    def second_gelu(u):
        q, p = divmod(u, pairs)
        a2[u], both, tail = gelu_parts(v2.pop(u))
        cot = jnp.concatenate([
            jnp.broadcast_to(cot_ref[2 * p + k : 2 * p + k + 1, q * chunk : (q + 1) * chunk], (hidden, chunk))
            for k in range(2)], axis=0)
        d2[u] = (cot * (both + tail.astype(f32))).astype(bf16)

    def third(u):
        q, p = divmod(u, pairs)
        back[u] = jnp.dot(w2t[...], d2[u], preferred_element_type=f32)
        part = jnp.dot(rox[p], a2[u], preferred_element_type=f32)
        cols = slice(q * chunk, (q + 1) * chunk)
        if p == 0:
            pred_ref[:, cols] = part + rb_ref[0, 0]
        else:
            pred_ref[:, cols] += part
        if u % joint == joint - 1:
            mine = range(u - joint + 1, u + 1)
            acc2[...] += lax.dot_general(
                jnp.concatenate([d2.pop(k) for k in mine], axis=1), jnp.concatenate([a1.pop(k) for k in mine], axis=1),
                NT, preferred_element_type=f32)

    def third_slope(u):
        d1[u] = (back.pop(u) * s1.pop(u)).astype(bf16)

    def fourth(u):
        if u % joint == joint - 1:
            mine = range(u - joint + 1, u + 1)
            both = [jnp.concatenate([d1.pop(k), a2.pop(k)], axis=0) for k in mine]
            acc1[...] += lax.dot_general(
                jnp.concatenate([x_of(k) for k in mine], axis=1), jnp.concatenate(both, axis=1),
                NT, preferred_element_type=f32)

    for i in range(-3, units + 3):
        if (i + 3) % pairs == 2 and (i + 3) // pairs + 1 < chunks:
            prepare((i + 3) // pairs + 1)
        for stage, lag in ((first, 3), (second_gelu, 0), (second, 1), (first_gelu, 2), (third, -1), (third_slope, -2),
                           (fourth, -3)):
            if 0 <= i + lag < units:
                stage(i + lag)

    @pl.when(step == pl.num_programs(0) - 1)
    def _():
        total2 = acc2[...]
        g2 = total2[0:hidden, 0:hidden] + total2[hidden:pair, hidden:pair]
        ro = jnp.sum((iota((hidden, hidden), 0) == iota((hidden, hidden), 1)).astype(f32) * ro_ref[...].astype(f32),
                     axis=1, keepdims=True)
        g2 = 0.25 * ro * g2
        bias = 0.5 * ro * (total2[0:hidden, pair : pair + 1] + total2[hidden:pair, pair : pair + 1])
        eye = iota((hidden, hidden), 0) == iota((hidden, hidden), 1)
        gb2 = jnp.sum(jnp.where(eye, bias, 0.0), axis=0, keepdims=True)
        flat = acc1[...]
        slot = iota((deep, pair), 0)
        side = iota((deep, pair), 1) // hidden
        keep = ((slot % 2 == side) & (slot < half)) | (slot == half)
        weights = jnp.where(keep, flat[:, 0:pair], 0.0)
        reads = jnp.where((slot % 2 == side) & (slot > half + 1), flat[:, pair : 2 * pair], 0.0)
        fold = (iota((pair, hidden), 0) % hidden == iota((pair, hidden), 1)).astype(f32)
        exact = dict(precision=lax.Precision.HIGHEST, preferred_element_type=f32)
        up = jnp.dot(weights, fold, **exact)
        up_r = jnp.dot(reads, fold, **exact)
        joined = jnp.where(iota((cin, deep), 1) // 2 == iota((cin, deep), 0), 1.0, 0.0)
        g1 = jnp.dot(joined, up, **exact)
        gb1 = up[half : half + 1]
        gr = 0.5 * jnp.sum(up_r, axis=0, keepdims=True)
        gb3 = jnp.broadcast_to(jnp.sum(accc[...], keepdims=True), (1, hidden))
        lines = jnp.concatenate([gb1, gr, gb2, gb3, jnp.zeros((cin - 4, hidden), f32)], axis=0)
        body = hidden // 2
        grads_ref[0:body] = jnp.concatenate([g2[0:body], g2[body:hidden]], axis=1)
        grads_ref[body : body + cin] = jnp.concatenate([g1, lines], axis=1)
        rest = grads_ref.shape[0] - body - cin
        grads_ref[body + cin :] = jnp.zeros((rest, 2 * hidden), f32)


def sum_rows(hidden):
    return (hidden // 2 + 8 + 15) // 16 * 16


def mlp(demand, base, feats, cot, w1, b1, w2, b2, ro, rb, width=2048, chunk=256):
    slab_rows, w = demand.shape
    hidden, cin = w1.shape
    packed = (sum_rows(hidden), 2 * hidden)
    pair = 2 * hidden
    depth = cin * slab_rows
    whole = lambda s: pl.BlockSpec(s, lambda i: tuple(0 for _ in s))
    cols = pl.BlockSpec((slab_rows, width), lambda i: (0, i))
    return pl.pallas_call(
        functools.partial(mlp_body, chunk),
        grid=(w // width,),
        in_specs=[
            cols, pl.BlockSpec((1, width), lambda i: (0, i)),
            pl.BlockSpec((cin - 1, slab_rows, width), lambda i: (0, 0, i)), cols,
            whole((cin, hidden)), whole((1, hidden)), whole((hidden, hidden)), whole((1, hidden)), whole((1, hidden)),
            pl.BlockSpec(memory_space=pltpu.SMEM),
        ],
        out_specs=[cols, whole(packed)],
        out_shape=[
            jax.ShapeDtypeStruct((slab_rows, w), f32),
            jax.ShapeDtypeStruct(packed, f32),
        ],
        scratch_shapes=[
            pltpu.VMEM((pair, 4 * cin), bf16),
            pltpu.VMEM((pair, pair + 128), bf16),
            pltpu.VMEM((pair, pair), bf16),
            pltpu.VMEM((slab_rows // 2, slab_rows, pair), bf16),
            pltpu.VMEM((2 * cin * slab_rows, depth + 3 * slab_rows), bf16),
            pltpu.VMEM((depth + 3 * slab_rows, width), bf16),
            pltpu.VMEM((2 * cin * slab_rows, width), bf16),
            pltpu.VMEM((4 * cin, 2 * pair), f32),
            pltpu.VMEM((pair, pair + slab_rows), f32),
            pltpu.VMEM((slab_rows, 128), f32),
        ],
        compiler_params=pltpu.CompilerParams(vmem_limit_bytes=vmem_most),
        name="mlp",
    )(demand, base, feats, cot, w1.T, b1[None, :], w2, b2[None, :], ro[None, :], rb[None, :])


def hail(n):
    me, group = lax.axis_index("canvas"), lax.axis_index("groups")
    barrier = pltpu.get_barrier_semaphore()

    def signal(k, carry):
        pl.semaphore_signal(
            barrier, inc=1, device_id=(group, lax.rem(me + k, n)), device_id_type=pl.DeviceIdType.MESH)
        return carry

    lax.fori_loop(1, n, signal, 0)


def all_here(n):
    pl.semaphore_wait(pltpu.get_barrier_semaphore(), n - 1)


def greet(n):
    hail(n)
    all_here(n)


def swap(n, source, target, send_sem, recv_sem):
    me, group = lax.axis_index("canvas"), lax.axis_index("groups")

    def copy(k, slot):
        peer = lax.rem(me + k, n)
        return pltpu.make_async_remote_copy(
            src_ref=source.at[peer], dst_ref=target.at[slot], send_sem=send_sem.at[k], recv_sem=recv_sem.at[k],
            device_id=(group, peer), device_id_type=pl.DeviceIdType.MESH)

    def start(k, carry):
        copy(k, me).start()
        return carry

    def arrive(k, carry):
        copy(k, lax.rem(me + n - k, n)).wait_recv()
        return carry

    lax.fori_loop(1, n, start, 0, unroll=True)
    target[pl.ds(me, 1)] = source[pl.ds(me, 1)]
    lax.fori_loop(1, n, arrive, 0, unroll=True)

    def finish():
        def left(k, carry):
            copy(k, me).wait_send()
            return carry

        lax.fori_loop(1, n, left, 0, unroll=True)

    return finish


def pack_items(n, slab_rows, w, slabs_ref, offsets_ref, left_ref, span_ref, pins_ref, send_ref):
    cap = send_ref.shape[2]
    one, two = slabs_ref[0:1, :], slabs_ref[1:2, :]
    off_one, off_two = offsets_ref[0:1, :], offsets_ref[1:2, :]
    first_is_low = one <= two
    low, high = jnp.minimum(one, two), jnp.maximum(one, two)
    low_row = jnp.where(first_is_low, off_one, off_two)
    high_row = jnp.where(first_is_low, off_two, off_one)
    left = left_ref[...]
    right = jnp.minimum(left + span_ref[...], w)
    wide = (right - left).astype(f32)
    tall = ((high - low) * slab_rows + high_row - low_row).astype(f32)
    weight = jnp.sqrt(pins_ref[...].astype(f32)) * (wide + tall) / (wide * tall)
    both = lambda x, y: jnp.concatenate([x, y], axis=1)
    slab = both(low, high)
    items = slab.shape[1]
    hot = jnp.where(iota((n, items), 0) == slab, 1.0, 0.0)
    hot_b = hot.astype(bf16)
    span = 256
    upper = (iota((span, span), 0) <= iota((span, span), 1)).astype(bf16)
    blocks = items // span
    before = ((iota((128, items), 1) // span) < iota((128, items), 0)).astype(bf16)
    starts = lax.dot_general(hot_b, before, NT, preferred_element_type=f32)
    counts = []
    for k in range(blocks):
        cols = slice(k * span, (k + 1) * span)
        inside = jnp.dot(hot_b[:, cols], upper, preferred_element_type=f32) + starts[:, k : k + 1]
        counts.append(jnp.sum(inside * hot[:, cols], axis=0, keepdims=True))
    rank = (jnp.concatenate(counts, axis=1) - 1.0).astype(i32)
    spot = jnp.where(iota((cap, items), 0) == rank, 1.0, 0.0).astype(bf16)
    amount = both(weight, -weight)
    coarse = amount.astype(bf16).astype(f32)
    row = both(low_row, high_row).astype(f32)
    start = both(left, left)
    end = both(right, right)
    start_low, end_low = start & 255, end & 255
    kind = iota((4 * n, items), 0) % 4
    mine = (iota((4 * n, items), 0) // 4) == slab

    def field(x0, x1, x2, x3):
        picked = jnp.where(kind == 0, x0, jnp.where(kind == 1, x1, jnp.where(kind == 2, x2, x3)))
        return jnp.where(mine, picked, 0.0).astype(bf16)

    big = field(coarse, row, (start - start_low).astype(f32), (end - end_low).astype(f32))
    small = field(amount - coarse, jnp.zeros_like(row), start_low.astype(f32), end_low.astype(f32))
    table = (lax.dot_general(big, spot, NT, preferred_element_type=f32)
             + lax.dot_general(small, spot, NT, preferred_element_type=f32))
    for d in range(n):
        send_ref[d] = table[4 * d : 4 * d + 4]


def slab(got_ref, local_ref, totals_ref, acc):
    n, _, cap = got_ref.shape
    slab_rows, w = local_ref.shape
    window = 256
    stride = window - 16
    tall = acc.shape[0]
    per = max(1, min(n, 2048 // cap))
    for c in range(n // per):
        def line(which):
            return jnp.concatenate([got_ref[c * per + j, which : which + 1, :] for j in range(per)], axis=1)

        value = line(0).astype(bf16)
        start = line(2)
        group = jnp.floor((start + 0.5) * (1.0 / stride))
        shift = group * stride
        first = (start - shift).astype(bf16)
        last = (line(3) - shift).astype(bf16)
        count = per * cap
        group = jnp.broadcast_to(group, (slab_rows, count)).astype(bf16)
        own_row = jnp.where(iota((slab_rows, count), 0).astype(f32) == line(1), 1.0, 0.0).astype(bf16)
        zero = jnp.zeros((slab_rows, count), bf16)
        hot = jnp.concatenate(
            [jnp.where(group == bf16(g), own_row, zero) for g in range(tall // slab_rows)], axis=0)
        lane = iota((window, count), 0).astype(f32).astype(bf16)
        fine = jnp.where((lane >= first) & (lane < last), value, jnp.zeros((window, count), bf16))
        update = lax.dot_general(hot, fine, NT, preferred_element_type=f32)
        if c == 0:
            acc[...] = update
        else:
            acc[...] += update
    tiles = [None] * (w // 128 + 4)
    for g in range(tall // slab_rows):
        at, turn = divmod(g * stride, 128)
        part = jnp.concatenate(
            [acc[g * slab_rows : (g + 1) * slab_rows, :], jnp.zeros((slab_rows, 128), f32)], axis=1)
        if turn:
            part = pltpu.roll(part, turn, 1)
        for k in range(3):
            piece = part[:, k * 128 : (k + 1) * 128]
            tiles[at + k] = piece if tiles[at + k] is None else tiles[at + k] + piece
    rows = iota((slab_rows, 128), 0)
    part = w // n
    for j in range(w // 128):
        t = tiles[j]
        step = 1
        while step < slab_rows:
            t = t + jnp.where(rows >= step, pltpu.roll(t, step, 0), 0.0)
            step *= 2
        local_ref[:, j * 128 : (j + 1) * 128] = t
    for d in range(n):
        totals_ref[d] = local_ref[slab_rows - 1 : slab_rows, d * part : (d + 1) * part]


def route_body(n, slabs_ref, offsets_ref, left_ref, span_ref, pins_ref, local_ref, base_ref,
               send, items, acc, totals, got, result, back, send_a, recv_a, send_b, recv_b, send_c, recv_c):
    hail(n)
    slab_rows, w = local_ref.shape
    pack_items(n, slab_rows, w, slabs_ref, offsets_ref, left_ref, span_ref, pins_ref, send)
    all_here(n)
    end_a = swap(n, send, items, send_a, recv_a)
    slab(items, local_ref, totals, acc)
    end_b = swap(n, totals, got, send_b, recv_b)
    running = jnp.zeros(got.shape[1:], f32)
    for d in range(n):
        result[d] = running
        running = running + got[d]
    end_c = swap(n, result, back, send_c, recv_c)
    part = got.shape[2]
    for d in range(n):
        base_ref[:, d * part : (d + 1) * part] = back[d]
    end_a()
    end_b()
    end_c()


def route(n, slabs, offsets, left, span, pins, slab_rows, w):
    cap = 4 * pins.shape[1] // n
    vmem = pl.BlockSpec(memory_space=pltpu.VMEM)
    part = pltpu.VMEM((n, 1, w // n), f32)
    groups = -(-w // 240)
    return pl.pallas_call(
        functools.partial(route_body, n),
        out_shape=[jax.ShapeDtypeStruct((slab_rows, w), f32), jax.ShapeDtypeStruct((1, w), f32)],
        in_specs=[vmem] * 5,
        out_specs=[vmem] * 2,
        scratch_shapes=[
            pltpu.VMEM((n, 4, cap), f32), pltpu.VMEM((n, 4, cap), f32), pltpu.VMEM((groups * slab_rows, 256), f32),
            part, part, part, part,
        ] + [pltpu.SemaphoreType.DMA((n,))] * 6,
        compiler_params=pltpu.CompilerParams(
            collective_id=0, has_side_effects=True, vmem_limit_bytes=vmem_most),
        name="route",
    )(slabs, offsets, left, span, pins)


def sum_body(n, grads_ref, total_ref, sibling, mine, halves, full, send_sem, recv_sem, pair_send, pair_recv):
    me, group = lax.axis_index("canvas"), lax.axis_index("groups")
    core = lax.rem(me, 2)
    chip = me // 2
    other = me + 1 - 2 * core
    chips = n // 2
    rows = halves.shape[1]
    barrier = pltpu.get_barrier_semaphore()

    def friend(k):
        return 2 * lax.rem(chip + k, chips) + core

    def signal(k, carry):
        pl.semaphore_signal(barrier, inc=1, device_id=(group, friend(k)), device_id_type=pl.DeviceIdType.MESH)
        return carry

    pl.semaphore_signal(barrier, inc=1, device_id=(group, other), device_id_type=pl.DeviceIdType.MESH)
    lax.fori_loop(1, chips, signal, 0)
    pl.semaphore_wait(barrier, chips)

    def hand(source, target, which):
        return pltpu.make_async_remote_copy(
            src_ref=source, dst_ref=target, send_sem=pair_send.at[which], recv_sem=pair_recv.at[which],
            device_id=(group, other), device_id_type=pl.DeviceIdType.MESH)

    first = hand(grads_ref, sibling, 0)
    first.start()
    first.wait_recv()
    mine[...] = grads_ref[...] + sibling[...]
    part = pl.ds(pl.multiple_of(core * rows, 8), rows)

    def copy(k, slot):
        return pltpu.make_async_remote_copy(
            src_ref=mine.at[part], dst_ref=halves.at[slot], send_sem=send_sem.at[k], recv_sem=recv_sem.at[k],
            device_id=(group, friend(k)), device_id_type=pl.DeviceIdType.MESH)

    def start(k, carry):
        copy(k, chip).start()
        return carry

    def arrive(k, carry):
        copy(k, lax.rem(chip + chips - k, chips)).wait_recv()
        return carry

    lax.fori_loop(1, chips, start, 0)
    halves[pl.ds(chip, 1)] = mine[part][None]
    lax.fori_loop(1, chips, arrive, 0)
    total = halves[0]
    for d in range(1, chips):
        total = total + halves[d]
    full[part] = total
    last = hand(full.at[part], full.at[part], 1)
    last.start()

    def left(k, carry):
        copy(k, chip).wait_send()
        return carry

    lax.fori_loop(1, chips, left, 0)
    first.wait_send()
    last.wait()
    total_ref[...] = full[...]


def split_body(cin, total_ref, g1_out, gb1_out, g2_out, gb2_out, gr_out, gb_out,
               g1_ref, gb1_ref, g2_ref, gb2_ref, gr_ref, gb_ref, out_sem):
    hidden = g1_ref.shape[1]
    body = hidden // 2
    g2_ref[0:body] = total_ref[0:body, 0:hidden]
    g2_ref[body:hidden] = total_ref[0:body, hidden:]
    g1_ref[...] = total_ref[body : body + cin, 0:hidden]
    for k, target in enumerate((gb1_ref, gr_ref, gb2_ref)):
        target[...] = total_ref[body + k : body + k + 1, hidden:].reshape(hidden)
    gb_ref[...] = total_ref[body + 3 : body + 4, hidden : hidden + 1].reshape(1)
    pairs = ((g1_ref, g1_out), (gb1_ref, gb1_out), (g2_ref, g2_out), (gb2_ref, gb2_out), (gr_ref, gr_out),
             (gb_ref, gb_out))
    copies = [pltpu.make_async_copy(source, target, out_sem.at[i]) for i, (source, target) in enumerate(pairs)]
    for c in copies:
        c.start()
    for c in copies:
        c.wait()


def sum_all(grads, n, shape):
    hidden, cin = shape
    vmem = pl.BlockSpec(memory_space=pltpu.VMEM)
    line = (hidden,)
    shapes = ((cin, hidden), line, (hidden, hidden), line, line, (1,))
    whole = pltpu.VMEM(grads.shape, f32)
    total = pl.pallas_call(
        functools.partial(sum_body, n),
        out_shape=jax.ShapeDtypeStruct(grads.shape, f32),
        in_specs=[vmem],
        out_specs=vmem,
        scratch_shapes=[whole, whole, pltpu.VMEM((n // 2, grads.shape[0] // 2, grads.shape[1]), f32), whole]
        + [pltpu.SemaphoreType.DMA((n // 2,))] * 2 + [pltpu.SemaphoreType.DMA((2,))] * 2,
        compiler_params=pltpu.CompilerParams(collective_id=1, has_side_effects=True),
        name="sum_all",
    )(grads)
    return pl.pallas_call(
        functools.partial(split_body, cin),
        out_shape=[jax.ShapeDtypeStruct(shape, f32) for shape in shapes],
        in_specs=[vmem],
        out_specs=[pl.BlockSpec(memory_space=pltpu.HBM)] * 6,
        scratch_shapes=[pltpu.VMEM(shape, f32) for shape in shapes] + [pltpu.SemaphoreType.DMA((6,))],
        name="split",
    )(total)


def per_device(
    net_slabs,
    row_offsets,
    left_column,
    column_span,
    pin_counts,
    tile_features,
    cotangent,
    first_weight,
    first_bias,
    second_weight,
    second_bias,
    readout_weight,
    readout_bias,
):
    devices = lax.axis_size("canvas")
    slab_rows = tile_features.shape[1]
    canvas_width = tile_features.shape[2]
    local, base = route(
        devices, net_slabs.T, row_offsets.T, left_column[None, :], column_span[None, :], pin_counts[None, :],
        slab_rows, canvas_width)
    prediction, grads = mlp(
        local, base, tile_features, cotangent, first_weight, first_bias, second_weight, second_bias,
        readout_weight, readout_bias)
    g1, gb1, g2, gb2, gr, gb = sum_all(grads, devices, first_weight.shape)
    return (prediction, g1.T, gb1, g2, gb2, gr, gb)


def solution(mesh):
    in_specs = (
        P(("groups", "canvas"), None),
        P(("groups", "canvas"), None),
        P(("groups", "canvas")),
        P(("groups", "canvas")),
        P(("groups", "canvas")),
        P(None, ("groups", "canvas"), None),
        P(("groups", "canvas"), None),
        P(),
        P(),
        P(),
        P(),
        P(),
        P(),
    )
    out_specs = (
        P(("groups", "canvas"), None),
        P("groups", None),
        P("groups"),
        P("groups", None),
        P("groups"),
        P("groups"),
        P("groups"),
    )
    return jax.shard_map(
        per_device, mesh=mesh, in_specs=in_specs, out_specs=out_specs, check_vma=False
    )
```
